32 devices in a mesh: mp: 4 (over x, core), dp: 8 (over z, y).
Axes of the slice: x: 2, y: 2, z: 4, core: 2. Of those that a mesh axis runs over, the one named last changes fastest.
Arguments:
- tokens: bfloat16 [128, 64, 1024], P('dp'), may hold values from -10 to 10
- norm_gain: float32 [1024], replicated, may hold values from 0.1 to 1.9
- weight_in: bfloat16 [1024, 4096], P(None, 'mp'), may hold values from -0.1875 to 0.1875
- weight_out: bfloat16 [4096, 1024], P('mp'), may hold values from -0.09375 to 0.09375
- final_gain: float32 [1024], replicated, may hold values from 0.1 to 1.9
- centres: bfloat16 [262144, 1024], P(('mp', 'dp')), may hold values from -7 to 7
- labels: int32 [128], P('dp'), may hold values from 0 to 262143
Outputs:
- row_loss: float32 [128], P('dp')
- feat_grad: float32 [128, 1024], P('dp', 'mp')
The draws below stay inside these ranges and needn't reach their ends.
All inputs are finite; a program needn't handle non-finite values.
Results may differ from the reference program's by a relative error of at most 0.0038.
Values may be sent and summed in bfloat16 or wider, within the bound.
A program may use at most 128 MiB of HBM per device.

```python
import math
import jax
import jax.numpy as jnp
from jax import lax

D = 1024
FF = 4096
CLS_DEV = 8192
TOK = 64
IMAGES = 128
CLASSES = 262144


def group_table(key):
    group_count = max(CLASSES // 256, 1)
    return jax.random.truncated_normal(jax.random.fold_in(key, 101), -4.0, 4.0, (group_count, D), jnp.float32)


def draw_tokens(key, part):
    table = group_table(key)
    group_count = table.shape[0]
    image_group = jax.random.randint(jax.random.fold_in(key, 103), (IMAGES,), 0, group_count).astype(jnp.int32)
    noise = jax.random.truncated_normal(jax.random.fold_in(key, 104), -4.0, 4.0, (IMAGES, TOK, D), jnp.float32)
    strength = jax.random.uniform(jax.random.fold_in(key, 105), (IMAGES,), jnp.float32, 0.0, 0.3)
    direction = table[image_group] * strength[:, None]
    return (noise + direction[:, None, :]).astype(jnp.bfloat16)


def draw_centres(key, part):
    table = group_table(key)
    group_count = table.shape[0]
    member_order = jax.random.permutation(jax.random.fold_in(key, 106), CLASSES).astype(jnp.int32)
    class_group = (member_order % group_count).astype(jnp.int32)
    block_count = CLASSES // CLS_DEV
    group_blocks = class_group.reshape(block_count, CLS_DEV)
    block_index = jnp.arange(block_count).astype(jnp.int32)
    block_key = jax.random.fold_in(key, 107)
    common = 0.26 * jax.random.truncated_normal(jax.random.fold_in(key, 108), -2.5, 2.5, (D,), jnp.float32)

    def one_block(inputs):
        block_groups, index = inputs
        sub_key = jax.random.fold_in(block_key, index)
        noise = jax.random.truncated_normal(jax.random.fold_in(sub_key, 1), -4.0, 4.0, (CLS_DEV, D), jnp.float32)
        pull = jax.random.uniform(jax.random.fold_in(sub_key, 2), (CLS_DEV,), jnp.float32, 0.0, 0.1)
        return noise + pull[:, None] * table[block_groups] + common[None, :]
    return lax.map(one_block, (group_blocks, block_index)).reshape(CLASSES, D).astype(jnp.bfloat16)


def plant(array, own_key, smallest, high):
    shape = array.shape
    index_at = [jax.random.randint(jax.random.fold_in(own_key, axis), (), 0, shape[axis]) for axis in range(len(shape))]
    array = array.at[tuple(index_at)].set(smallest)
    longest = shape.index(max(shape))
    index_at[longest] = (index_at[longest] + 1) % shape[longest]
    return array.at[tuple(index_at)].set(high)


def levels(stream_key, shape, cuts, least, top_value):
    factor_of, own = 1.0, jax.random.fold_in(stream_key, 6)
    for position, parts in cuts:
        heights = jnp.exp(jax.random.uniform(jax.random.fold_in(own, position), (parts,), jnp.float32, least / len(cuts), top_value / len(cuts)))
        factor_of = factor_of * jnp.repeat(heights, shape[position] // parts).reshape([-1 if axis == position else 1 for axis in range(len(shape))])
    return factor_of


def scatter_about(stream_key, shape, deviation, bound, pieces=(), held_as=jnp.bfloat16):
    array = jax.random.normal(stream_key, shape, jnp.float32) * deviation
    if len(pieces) > 0:
        array = levels(stream_key, shape, pieces, -0.22, 0.18) * array
    return jnp.clip(array, min=-bound, max=bound).astype(held_as)


def setup_inputs(seed: int = 0) -> dict:
    streams_of = jax.random.split(jax.random.key(seed), 8)
    return {
        "tokens": draw_tokens(jax.random.fold_in(streams_of[7], 71), 0),
        "norm_gain": jnp.clip(1.0 + 0.18 * jax.random.normal(streams_of[1], (D,), jnp.float32), 0.1, 1.9),
        "weight_in": scatter_about(streams_of[2], (D, FF), D ** -0.5, 0.1875, ((1, 4),)),
        "weight_out": scatter_about(streams_of[3], (FF, D), FF ** -0.5, 0.09375, ((0, 4),)),
        "final_gain": jnp.clip(1.0 + 0.18 * jax.random.normal(streams_of[4], (D,), jnp.float32), 0.1, 1.9),
        "centres": draw_centres(jax.random.fold_in(streams_of[7], 71), 0),
        "labels": plant(jax.random.randint(streams_of[6], (IMAGES,), 0, CLASSES), jax.random.fold_in(streams_of[6], 1), 0, CLASSES - 1).astype(jnp.int32),
    }


logit_scale = 64.0
angle_margin = 0.5

def layer_norm(values, gain_vec):
    average = lax.optimization_barrier(jnp.mean(values, axis=-1, keepdims=True))
    centred = values - average
    variance = lax.optimization_barrier(jnp.mean(centred * centred, axis=-1, keepdims=True))
    return centred * lax.rsqrt(variance + 1e-06) * gain_vec

def arc_target(target_cos):
    target_sine = jnp.sqrt(jnp.maximum(1.0 - target_cos * target_cos, 0.01))
    inside = target_cos > -math.cos(angle_margin)
    shifted = jnp.where(inside, target_cos * math.cos(angle_margin) - target_sine * math.sin(angle_margin), target_cos - angle_margin * math.sin(angle_margin))
    margin_slope = jnp.where(inside, math.cos(angle_margin) + math.sin(angle_margin) * target_cos / target_sine, 1.0)
    return (shifted, margin_slope)

def unit_centres(centre_block):
    block_wide = centre_block.astype(jnp.float32)
    return (block_wide * lax.rsqrt(lax.optimization_barrier(jnp.sum(block_wide * block_wide, axis=1, keepdims=True)) + 1e-06)).astype(jnp.bfloat16)

def block_logits(unit_rows, centre_unit, labels, offset):
    cosine = lax.dot_general(unit_rows, centre_unit, (((1,), (1,)), ((), ())), preferred_element_type=jnp.float32)
    local_label = labels - offset
    picked = local_label[:, None] == lax.broadcasted_iota(jnp.int32, cosine.shape, 1)
    target_cos = lax.optimization_barrier(jnp.sum(jnp.where(picked, cosine, 0.0), axis=1))
    shifted, margin_slope = arc_target(target_cos)
    logits = jnp.where(picked, logit_scale * shifted[:, None], logit_scale * cosine)
    is_owner = jnp.any(picked, axis=1)
    return (logits, picked, is_owner, shifted, margin_slope)

def reference(tokens, norm_gain, weight_in, weight_out, final_gain, centres, labels):
    model_width = tokens.shape[2]
    tokens_wide = tokens.astype(jnp.float32)
    normed = layer_norm(tokens_wide, norm_gain).astype(jnp.bfloat16).reshape(-1, model_width)
    hidden = jax.nn.gelu(jnp.dot(normed, weight_in, preferred_element_type=jnp.float32), approximate=False).astype(jnp.bfloat16)
    branch = jnp.dot(hidden, weight_out, preferred_element_type=jnp.float32).reshape(tokens.shape)
    pooled = lax.optimization_barrier(jnp.mean(tokens_wide, axis=1)) + lax.optimization_barrier(jnp.mean(branch, axis=1))
    embedding = layer_norm(pooled, final_gain)
    length = jnp.sqrt(lax.optimization_barrier(jnp.sum(embedding * embedding, axis=1)) + 1e-06)
    unit_rows = (embedding / length[:, None]).astype(jnp.bfloat16)
    blocks = centres.reshape(-1, CLS_DEV, model_width)
    block_ids = jnp.arange(blocks.shape[0]).astype(jnp.int32)

    def first_pass(carried, inputs):
        centre_block, block_index = inputs
        offset = (block_index * CLS_DEV).astype(jnp.int32)
        logits, picked, is_owner, shifted, margin_slope = block_logits(unit_rows, unit_centres(centre_block), labels, offset)
        totals = carried[0] + lax.optimization_barrier(jnp.sum(jnp.exp(logits), axis=1))
        target = carried[1] + jnp.where(is_owner, logit_scale * shifted, 0.0)
        return ((totals, target), None)
    zeros_rows = jnp.zeros((unit_rows.shape[0],), jnp.float32)
    (totals, target), _ = lax.scan(first_pass, (zeros_rows, zeros_rows), (blocks, block_ids))
    row_loss = jnp.log(totals) - target

    def second_pass(carried, inputs):
        centre_block, block_index = inputs
        offset = (block_index * CLS_DEV).astype(jnp.int32)
        centre_unit = unit_centres(centre_block)
        logits, picked, is_owner, shifted, margin_slope = block_logits(unit_rows, centre_unit, labels, offset)
        probability = jnp.exp(logits) / totals[:, None]
        weights = (logit_scale * jnp.where(picked, (probability - 1.0) * margin_slope[:, None], probability)).astype(jnp.bfloat16)
        return (carried + jnp.dot(weights, centre_unit, preferred_element_type=jnp.float32), None)
    grad_unit, _ = lax.scan(second_pass, jnp.zeros(unit_rows.shape, jnp.float32), (blocks, block_ids))
    unit_wide = unit_rows.astype(jnp.float32)
    inner_dots = lax.optimization_barrier(jnp.sum(unit_wide * grad_unit, axis=1))
    feat_grad = (grad_unit - unit_wide * inner_dots[:, None]) / length[:, None]
    return (row_loss, feat_grad)
```

```python
import functools
import math

import jax
import jax.numpy as jnp
from jax import lax
from jax.experimental import pallas as pl
from jax.experimental.pallas import tpu as pltpu
from jax.sharding import PartitionSpec as P

logit_scale = 64.0
angle_margin = 0.5
MESH = pl.DeviceIdType.MESH
F32 = jnp.float32
BF16 = jnp.bfloat16
STATS = 4
SUBLANES = 8


def layer_norm(values, gain_vec):
    average = jnp.mean(values, axis=-1, keepdims=True)
    centred = values - average
    variance = jnp.mean(centred * centred, axis=-1, keepdims=True)
    return centred * lax.rsqrt(variance + 1e-06) * gain_vec


def arc_target(target_cos):
    target_sine = jnp.sqrt(jnp.maximum(1.0 - target_cos * target_cos, 0.01))
    inside = target_cos > -math.cos(angle_margin)
    shifted = jnp.where(
        inside,
        target_cos * math.cos(angle_margin) - target_sine * math.sin(angle_margin),
        target_cos - angle_margin * math.sin(angle_margin),
    )
    margin_slope = jnp.where(
        inside, math.cos(angle_margin) + math.sin(angle_margin) * target_cos / target_sine, 1.0
    )
    return (shifted, margin_slope)


def fold_lanes(values):
    total = values[:, 0:128]
    for start in range(128, values.shape[1], 128):
        total = total + values[:, start : start + 128]
    return total


def nt_dot(left, right):
    return lax.dot_general(left, right, (((1,), (1,)), ((), ())), preferred_element_type=F32)


def kernel(
    n_mp, n_dp, chunk, group,
    tokens_hbm, gain_ref, win_hbm, wout_hbm, final_ref, centres_hbm, labels_ref,
    loss_ref, grad_ref,
    tokens, win, wout, centres, labs, hid_sum, tok_sum, part, part_in, units, unit_full, rows_all,
    scales, picked_rows, weights, stat_own, stat_pair, stat_out, stat_in, stat_sum,
    pick_pass, pick_pair, pick_out, pick_in, grad_pass, grad_pair, grad_out, grad_in, lab_out,
    tok_sem, w_sem, c_sem, send_sem, lab_sem, part_sem, unit_sem, fwd_sem, stat_pair_sem, stat_sem,
    pick_pair_sem, pick_sem, grad_pair_sem, grad_sem,
):
    n_half = n_mp // 2
    n_chip = n_half * n_dp
    mp, dp = lax.axis_index("mp"), lax.axis_index("dp")
    me = mp * n_dp + dp
    core, side = lax.rem(mp, 2), mp // 2
    chip = side * n_dp + dp
    sibling = {"mp": mp + 1 - 2 * core, "dp": dp}
    images, tok_count, width = tokens.shape
    every = images * n_dp
    classes = centres.shape[0]
    n_chunk = classes // chunk
    cols = width // n_mp
    half = width // 2
    offset = me * classes

    def at_chip(index):
        return {"mp": 2 * (index // n_dp) + core, "dp": lax.rem(index, n_dp)}

    def get_group(index):
        return pltpu.make_async_copy(
            tokens_hbm.at[pl.ds(index * group, group)],
            tokens.at[pl.ds(index * group, group)],
            tok_sem.at[index],
        )

    def get_chunk(index):
        here = pl.ds(pl.multiple_of(index * chunk, chunk), chunk)
        return pltpu.make_async_copy(centres_hbm.at[here], centres.at[here], c_sem.at[index])

    get_win = pltpu.make_async_copy(win_hbm, win, w_sem.at[0])
    get_wout = pltpu.make_async_copy(wout_hbm, wout, w_sem.at[1])
    get_group(0).start()
    get_win.start()
    for index in range(1, images // group):
        get_group(index).start()
    get_wout.start()

    @pl.loop(0, n_chunk)
    def _(index):
        get_chunk(index).start()

    barrier = pltpu.get_barrier_semaphore()

    @pl.loop(1, n_chip)
    def _(step):
        peer = at_chip(lax.rem(chip + step, n_chip))
        pl.semaphore_signal(barrier, inc=1, device_id=peer, device_id_type=MESH)

    @pl.loop(0, n_half)
    def _(step):
        peer = {"mp": 2 * step + 1 - core, "dp": dp}
        pl.semaphore_signal(barrier, inc=1, device_id=peer, device_id_type=MESH)

    image_id = lax.broadcasted_iota(jnp.int32, (images, 128), 0)
    label_lanes = jnp.zeros((images, 128), jnp.int32)
    for index in range(images):
        label_lanes = jnp.where(image_id == index, labels_ref[index], label_lanes)
    lab_out[...] = label_lanes
    get_win.wait()

    def feed_group(index, carry):
        get_group(index).wait()
        wide = tokens[pl.ds(index * group, group)].astype(F32)
        here = pl.ds(pl.multiple_of(index * group, group), group)
        tok_sum[here, :] = jnp.sum(wide, axis=1)
        flat = wide.reshape(group * tok_count, width)
        normed = layer_norm(flat, gain_ref[...]).astype(BF16)
        pre = jnp.dot(normed, win[...], preferred_element_type=F32)
        hidden = 0.5 * pre * (1.0 + lax.erf(pre * math.sqrt(0.5)))
        hidden = hidden.astype(BF16).astype(F32).reshape(group, tok_count, pre.shape[1])
        hid_sum[here, :] = jnp.sum(hidden, axis=1)
        return carry

    lax.fori_loop(0, images // group, feed_group, 0)

    pl.semaphore_wait(barrier, n_chip - 1 + n_half)

    def label_copy(step):
        peer = lax.rem(dp + step, n_dp)
        return pltpu.make_async_remote_copy(
            src_ref=lab_out, dst_ref=labs.at[dp], send_sem=send_sem.at[0], recv_sem=lab_sem,
            device_id={"mp": mp, "dp": peer}, device_id_type=MESH,
        )

    def part_copy(step):
        peer = lax.rem(mp + step, n_mp)
        return pltpu.make_async_remote_copy(
            src_ref=part, dst_ref=part_in.at[mp], send_sem=send_sem.at[1], recv_sem=part_sem,
            device_id={"mp": peer, "dp": dp}, device_id_type=MESH,
        )

    def unit_copy(step):
        peer = lax.rem(dp + step, n_dp)
        return pltpu.make_async_remote_copy(
            src_ref=rows_all.at[core], dst_ref=units.at[core, dp],
            send_sem=send_sem.at[2], recv_sem=unit_sem,
            device_id={"mp": mp, "dp": peer}, device_id_type=MESH,
        )

    def unit_pass():
        return pltpu.make_async_remote_copy(
            src_ref=units.at[core], dst_ref=units.at[core],
            send_sem=send_sem.at[3], recv_sem=fwd_sem,
            device_id=sibling, device_id_type=MESH,
        )

    def stat_swap():
        return pltpu.make_async_remote_copy(
            src_ref=stat_own, dst_ref=stat_pair, send_sem=send_sem.at[4], recv_sem=stat_pair_sem,
            device_id=sibling, device_id_type=MESH,
        )

    def stat_copy(step):
        return pltpu.make_async_remote_copy(
            src_ref=stat_out, dst_ref=stat_in.at[chip], send_sem=send_sem.at[5], recv_sem=stat_sem,
            device_id=at_chip(lax.rem(chip + step, n_chip)), device_id_type=MESH,
        )

    def pick_swap():
        return pltpu.make_async_remote_copy(
            src_ref=pick_pass, dst_ref=pick_pair, send_sem=send_sem.at[6], recv_sem=pick_pair_sem,
            device_id=sibling, device_id_type=MESH,
        )

    def pick_copy(to):
        return pltpu.make_async_remote_copy(
            src_ref=pick_out.at[to // n_dp, lax.rem(to, n_dp)], dst_ref=pick_in.at[chip],
            send_sem=send_sem.at[7], recv_sem=pick_sem,
            device_id=at_chip(to), device_id_type=MESH,
        )

    def grad_swap(to):
        return pltpu.make_async_remote_copy(
            src_ref=grad_pass.at[to], dst_ref=grad_pair.at[to],
            send_sem=send_sem.at[8], recv_sem=grad_pair_sem.at[to],
            device_id=sibling, device_id_type=MESH,
        )

    def grad_copy(to):
        return pltpu.make_async_remote_copy(
            src_ref=grad_out.at[to // n_dp, lax.rem(to, n_dp)], dst_ref=grad_in.at[chip],
            send_sem=send_sem.at[9], recv_sem=grad_sem,
            device_id=at_chip(to), device_id_type=MESH,
        )

    def wait_bytes(ref, count, sem):
        pltpu.make_async_copy(ref.at[pl.ds(0, count)], ref.at[pl.ds(0, count)], sem).wait()

    get_wout.wait()
    hid_mean = hid_sum[...] * (1.0 / tok_count)
    high = hid_mean.astype(BF16)
    low = (hid_mean - high.astype(F32)).astype(BF16)
    both = jnp.dot(jnp.concatenate([high, low], axis=0), wout[...], preferred_element_type=F32)
    own_part = (both[0:images] + both[images:]).astype(BF16)
    part[...] = own_part

    @pl.loop(1, n_mp)
    def _(step):
        part_copy(lax.rem(step + 1, n_mp - 1) + 1).start()

    @pl.loop(1, n_dp)
    def _(step):
        label_copy(step).start()

    part_in[mp] = own_part
    labs[dp] = label_lanes
    ones = jnp.ones((SUBLANES, 128), BF16)

    def scale_chunk(index, carry):
        get_chunk(index).wait()
        here = pl.ds(pl.multiple_of(index * chunk, chunk), chunk)
        squares = None
        for start in range(0, width, 128):
            piece = centres[here, start : start + 128].astype(F32)
            squares = piece * piece if squares is None else squares + piece * piece
        high = squares.astype(BF16)
        low = (squares - high.astype(F32)).astype(BF16)
        scales[:, here] = lax.rsqrt(nt_dot(ones, high) + nt_dot(ones, low) + 1e-06)
        return carry

    lax.fori_loop(0, n_chunk // 2, scale_chunk, 0)

    wait_bytes(part_in, n_mp - 1, part_sem)
    pooled = tok_sum[...] * (1.0 / tok_count) + jnp.sum(part_in[...].astype(F32), axis=0)
    embedding = layer_norm(pooled, final_ref[...])
    length = jnp.sqrt(jnp.sum(embedding * embedding, axis=1, keepdims=True) + 1e-06)
    own_rows = (embedding / length).astype(BF16)
    rows_all[0] = own_rows[:, 0:half]
    rows_all[1] = own_rows[:, half:]

    @pl.loop(0, n_dp)
    def _(step):
        hop = lax.rem(n_dp // 2 + step, n_dp)

        @pl.when(hop != 0)
        def _():
            unit_copy(hop).start()

    units[core, dp] = rows_all[core]
    lax.fori_loop(n_chunk // 2, n_chunk, scale_chunk, 0)

    wait_bytes(labs, n_dp - 1, lab_sem)
    local_label = labs[...].reshape(every, 128)[:, 0:1] - offset

    def pick(index):
        lane = lax.broadcasted_iota(jnp.int32, (every, chunk), 1) + index * chunk
        return lane == local_label

    picked_rows[...] = jnp.zeros_like(picked_rows)

    def pick_chunk(index, carry):
        here = pl.ds(pl.multiple_of(index * chunk, chunk), chunk)
        picked = pick(index)
        picked_rows[...] += jnp.dot(
            jnp.where(picked, 1.0, 0.0).astype(BF16), centres[here, :], preferred_element_type=F32
        )
        return carry + fold_lanes(jnp.where(picked, scales[0:1, here], 0.0))

    zeros = jnp.zeros((every, 128), F32)
    scale_lanes = lax.fori_loop(0, n_chunk, pick_chunk, zeros)
    own_scale = jnp.sum(scale_lanes, axis=1, keepdims=True)

    def pick_block(to_mp):
        here = pl.ds(pl.multiple_of(to_mp * cols, cols), cols)
        return (picked_rows[:, here] * own_scale).astype(BF16).reshape(n_dp, images, cols)

    for to in range(n_half):
        pick_pass[to] = pick_block(2 * to + 1 - core)
    pick_swap().start()

    wait_bytes(units.at[core], n_dp - 1, unit_sem)
    unit_pass().start()

    pick_swap().wait_recv()
    for to in range(n_half):
        pick_out[to] = pick_block(2 * to + core) + pick_pair[to]

    @pl.loop(1, n_chip)
    def _(step):
        pick_copy(lax.rem(chip + step, n_chip)).start()

    pick_in[chip] = pick_out[side, dp]
    unit_pass().wait_recv()
    unit_full[:, 0:half] = units[0].reshape(every, half)
    unit_full[:, half:] = units[1].reshape(every, half)

    def class_chunk(index, carry):
        total, inner, target = carry
        here = pl.ds(pl.multiple_of(index * chunk, chunk), chunk)
        raw = nt_dot(unit_full[...], centres[here, :])
        scale = scales[0:1, here]
        cosine = raw * scale
        picked = pick(index)
        exponent = jnp.where(picked, 0.0, jnp.exp(logit_scale * cosine))
        weight = (exponent * scale).astype(BF16)
        weights[:, here] = weight
        return (
            total + fold_lanes(exponent),
            inner + fold_lanes(weight.astype(F32) * raw),
            target + fold_lanes(jnp.where(picked, cosine, 0.0)),
        )

    total, inner, target = lax.fori_loop(0, n_chunk, class_chunk, (zeros, zeros, zeros))
    lane = lax.broadcasted_iota(jnp.int32, (every, 128), 1)
    packed = jnp.where(
        lane == 0,
        jnp.sum(total, axis=1, keepdims=True),
        jnp.where(
            lane == 1,
            jnp.sum(inner, axis=1, keepdims=True),
            jnp.where(lane == 2, jnp.sum(target, axis=1, keepdims=True), 0.0),
        ),
    )
    stat_own[...] = packed.T[0:STATS, :]
    stat_swap().start()

    def grad_block(to_mp):
        here = pl.ds(pl.multiple_of(to_mp * cols, cols), cols)
        return jnp.dot(weights[...], centres[:, here], preferred_element_type=F32)

    def pass_cols(step, carry):
        to = lax.rem(side + 1 + step, n_half)
        block = grad_block(2 * to + 1 - core)
        grad_pass[to] = block.astype(BF16).reshape(n_dp, images, cols)
        grad_swap(to).start()
        return carry

    lax.fori_loop(0, n_half, pass_cols, 0)

    stat_swap().wait_recv()
    chip_stats = stat_own[...] + stat_pair[...]
    stat_out[...] = chip_stats

    @pl.loop(1, n_chip)
    def _(step):
        stat_copy(step).start()

    stat_in[chip] = chip_stats

    def send_cols(step, carry):
        to = lax.rem(side + 1 + step, n_half)
        grad_swap(to).wait_recv()
        block = grad_block(2 * to + core) + grad_pair[to].reshape(every, cols).astype(F32)
        grad_out[to] = block.astype(BF16).reshape(n_dp, images, cols)

        @pl.loop(0, n_dp)
        def _(hop):
            peer = to * n_dp + lax.rem(dp + n_dp // 2 + hop, n_dp)

            @pl.when(peer != chip)
            def _():
                grad_copy(peer).start()

        return carry

    lax.fori_loop(0, n_half, send_cols, 0)
    grad_in[chip] = grad_out[side, dp]

    wait_bytes(stat_in, n_chip - 1, stat_sem)
    stat_sum[...] = jnp.zeros_like(stat_sum)
    stat_sum[0:STATS, :] = jnp.sum(stat_in[...], axis=0)
    picked_rows[:, 0:128] = stat_sum[...].T
    stats = picked_rows[pl.ds(pl.multiple_of(dp * images, images), images), 0:128]
    others, inner_sum, target_cos = stats[:, 0:1], stats[:, 1:2], stats[:, 2:3]
    shifted, slope = arc_target(target_cos)
    target_exp = jnp.exp(logit_scale * shifted)
    totals = others + target_exp
    rate = logit_scale / totals
    target_weight = (logit_scale * ((target_exp / totals - 1.0) * slope)).astype(BF16).astype(F32)
    inner_all = rate * inner_sum + target_weight * target_cos
    diagonal = lax.broadcasted_iota(jnp.int32, (images, images), 0) == lax.broadcasted_iota(
        jnp.int32, (images, images), 1
    )
    row_loss = jnp.log(totals) - logit_scale * shifted
    loss_ref[...] = jnp.sum(jnp.where(diagonal, row_loss, 0.0), axis=0, keepdims=True)
    unit_here = unit_full[
        pl.ds(pl.multiple_of(dp * images, images), images),
        pl.ds(pl.multiple_of(mp * cols, cols), cols),
    ].astype(F32)
    wait_bytes(pick_in, n_chip - 1, pick_sem)
    centre_rows = jnp.sum(pick_in[...].astype(F32), axis=0)
    rest = target_weight * centre_rows - unit_here * inner_all
    wait_bytes(grad_in, n_chip - 1, grad_sem)
    gathered = jnp.sum(grad_in[...].astype(F32), axis=0)
    grad_ref[...] = (gathered * rate + rest) / length

    @pl.loop(1, n_mp)
    def _(step):
        part_copy(step).wait_send()

    @pl.loop(1, n_dp)
    def _(step):
        label_copy(step).wait_send()
        unit_copy(step).wait_send()

    unit_pass().wait_send()
    stat_swap().wait_send()
    pick_swap().wait_send()

    @pl.loop(0, n_half)
    def _(to):
        grad_swap(to).wait_send()

    @pl.loop(1, n_chip)
    def _(step):
        peer = lax.rem(chip + step, n_chip)
        stat_copy(step).wait_send()
        pick_copy(peer).wait_send()
        grad_copy(peer).wait_send()


def shards(n_mp, n_dp, tokens, norm_gain, weight_in, weight_out, final_gain, centres, labels):
    images, tok_count, width = tokens.shape
    hidden = weight_in.shape[1]
    classes = centres.shape[0]
    every = images * n_dp
    n_half = n_mp // 2
    n_chip = n_half * n_dp
    cols = width // n_mp
    chunk = min(1024, classes)
    group = 8
    any_spec = pl.BlockSpec(memory_space=pltpu.HBM)
    vmem_spec = pl.BlockSpec(memory_space=pltpu.VMEM)
    loss, grad = pl.pallas_call(
        functools.partial(kernel, n_mp, n_dp, chunk, group),
        out_shape=(
            jax.ShapeDtypeStruct((1, images), F32),
            jax.ShapeDtypeStruct((images, cols), F32),
        ),
        in_specs=[any_spec, vmem_spec, any_spec, any_spec, vmem_spec, any_spec,
            pl.BlockSpec(memory_space=pltpu.SMEM)],
        out_specs=(vmem_spec, vmem_spec),
        scratch_shapes=[
            pltpu.VMEM((images, tok_count, width), BF16),
            pltpu.VMEM((width, hidden), BF16),
            pltpu.VMEM((hidden, width), BF16),
            pltpu.VMEM((classes, width), BF16),
            pltpu.VMEM((n_dp, images, 128), jnp.int32),
            pltpu.VMEM((images, hidden), F32),
            pltpu.VMEM((images, width), F32),
            pltpu.VMEM((images, width), BF16),
            pltpu.VMEM((n_mp, images, width), BF16),
            pltpu.VMEM((2, n_dp, images, width // 2), BF16),
            pltpu.VMEM((every, width), BF16),
            pltpu.VMEM((2, images, width // 2), BF16),
            pltpu.VMEM((SUBLANES, classes), F32),
            pltpu.VMEM((every, width), F32),
            pltpu.VMEM((every, classes), BF16),
            pltpu.VMEM((STATS, every), F32),
            pltpu.VMEM((STATS, every), F32),
            pltpu.VMEM((STATS, every), F32),
            pltpu.VMEM((n_chip, STATS, every), F32),
            pltpu.VMEM((128, every), F32),
            pltpu.VMEM((n_half, n_dp, images, cols), BF16),
            pltpu.VMEM((n_half, n_dp, images, cols), BF16),
            pltpu.VMEM((n_half, n_dp, images, cols), BF16),
            pltpu.VMEM((n_chip, images, cols), BF16),
            pltpu.VMEM((n_half, n_dp, images, cols), BF16),
            pltpu.VMEM((n_half, n_dp, images, cols), BF16),
            pltpu.VMEM((n_half, n_dp, images, cols), BF16),
            pltpu.VMEM((n_chip, images, cols), BF16),
            pltpu.VMEM((images, 128), jnp.int32),
            pltpu.SemaphoreType.DMA((images // group,)),
            pltpu.SemaphoreType.DMA((2,)),
            pltpu.SemaphoreType.DMA((classes // chunk,)),
            pltpu.SemaphoreType.DMA((10,)),
            pltpu.SemaphoreType.DMA,
            pltpu.SemaphoreType.DMA,
            pltpu.SemaphoreType.DMA,
            pltpu.SemaphoreType.DMA,
            pltpu.SemaphoreType.DMA,
            pltpu.SemaphoreType.DMA,
            pltpu.SemaphoreType.DMA,
            pltpu.SemaphoreType.DMA,
            pltpu.SemaphoreType.DMA((n_half,)),
            pltpu.SemaphoreType.DMA,
        ],
        compiler_params=pltpu.CompilerParams(
            collective_id=0, has_side_effects=True, vmem_limit_bytes=56 * 1024 * 1024
        ),
    )(
        tokens, norm_gain.reshape(1, width), weight_in, weight_out,
        final_gain.reshape(1, width), centres, labels,
    )
    def emit(loss_in, grad_in, loss_out, grad_out):
        loss_out[...] = loss_in[...]
        grad_out[...] = grad_in[...]

    loss, grad = pl.pallas_call(
        emit,
        out_shape=(
            jax.ShapeDtypeStruct((1, images), F32),
            jax.ShapeDtypeStruct((images, cols), F32),
        ),
        in_specs=[vmem_spec, vmem_spec],
        out_specs=(vmem_spec, vmem_spec),
    )(loss, grad)
    return (loss.reshape(images), grad)


def solution(mesh):
    return jax.shard_map(
        functools.partial(shards, mesh.shape["mp"], mesh.shape["dp"]),
        mesh=mesh,
        in_specs=(
            P("dp", None, None),
            P(),
            P(None, "mp"),
            P("mp", None),
            P(),
            P(("mp", "dp"), None),
            P("dp"),
        ),
        out_specs=(P("dp"), P("dp", "mp")),
        check_vma=False,
    )
```

```python
import functools
import math

import jax
import jax.numpy as jnp
from jax import lax
from jax.experimental import pallas as pl
from jax.experimental.pallas import tpu as pltpu
from jax.sharding import PartitionSpec as P

logit_scale = 64.0
angle_margin = 0.5
MESH = pl.DeviceIdType.MESH
F32 = jnp.float32
BF16 = jnp.bfloat16
STATS = 4
SUBLANES = 8


def layer_norm(values, gain_vec):
    average = jnp.mean(values, axis=-1, keepdims=True)
    centred = values - average
    variance = jnp.mean(centred * centred, axis=-1, keepdims=True)
    return centred * lax.rsqrt(variance + 1e-06) * gain_vec


def arc_target(target_cos):
    target_sine = jnp.sqrt(jnp.maximum(1.0 - target_cos * target_cos, 0.01))
    inside = target_cos > -math.cos(angle_margin)
    shifted = jnp.where(
        inside,
        target_cos * math.cos(angle_margin) - target_sine * math.sin(angle_margin),
        target_cos - angle_margin * math.sin(angle_margin),
    )
    margin_slope = jnp.where(
        inside, math.cos(angle_margin) + math.sin(angle_margin) * target_cos / target_sine, 1.0
    )
    return (shifted, margin_slope)


def fold_rows(values):
    return jnp.sum(values.reshape(-1, SUBLANES, values.shape[1]), axis=0)


def nt_dot(left, right):
    return lax.dot_general(left, right, (((1,), (1,)), ((), ())), preferred_element_type=F32)


def kernel(
    n_mp, n_dp, chunk, group,
    tokens_hbm, gain_ref, win_hbm, wout_hbm, final_ref, centres_hbm, labels_ref,
    loss_ref, grad_ref,
    tokens, win, wout, centres, labs, hid_sum, tok_sum, part, part_in, units, unit_full, unit_t, raw_half, rows_all,
    scales, picked_rows, weights, stat_own, stat_pair, stat_out, stat_in, stat_sum,
    pick_pass, pick_pair, pick_out, pick_in, grad_pass, grad_pair, grad_out, grad_in, lab_out,
    tok_sem, w_sem, c_sem, send_sem, lab_sem, part_sem, unit_sem, fwd_sem, stat_pair_sem, stat_sem,
    pick_pair_sem, pick_sem, grad_pair_sem, grad_sem,
):
    n_half = n_mp // 2
    n_chip = n_half * n_dp
    mp, dp = lax.axis_index("mp"), lax.axis_index("dp")
    me = mp * n_dp + dp
    core, side = lax.rem(mp, 2), mp // 2
    chip = side * n_dp + dp
    sibling = {"mp": mp + 1 - 2 * core, "dp": dp}
    images, tok_count, width = tokens.shape
    every = images * n_dp
    classes = centres.shape[0]
    n_chunk = classes // chunk
    cols = width // n_mp
    half = width // 2
    offset = me * classes
    log_scale = logit_scale * math.log2(math.e)

    def at_chip(index):
        return {"mp": 2 * (index // n_dp) + core, "dp": lax.rem(index, n_dp)}

    def get_group(index):
        return pltpu.make_async_copy(
            tokens_hbm.at[pl.ds(index * group, group)],
            tokens.at[pl.ds(index * group, group)],
            tok_sem.at[index],
        )

    def get_chunk(index):
        here = pl.ds(pl.multiple_of(index * chunk, chunk), chunk)
        return pltpu.make_async_copy(centres_hbm.at[here], centres.at[here], c_sem.at[index])

    get_win = pltpu.make_async_copy(win_hbm, win, w_sem.at[0])
    get_wout = pltpu.make_async_copy(wout_hbm, wout, w_sem.at[1])
    get_group(0).start()
    get_win.start()
    for index in range(1, images // group):
        get_group(index).start()
    get_wout.start()

    @pl.loop(0, n_chunk)
    def _(index):
        get_chunk(index).start()

    barrier = pltpu.get_barrier_semaphore()

    @pl.loop(1, n_chip)
    def _(step):
        peer = at_chip(lax.rem(chip + step, n_chip))
        pl.semaphore_signal(barrier, inc=1, device_id=peer, device_id_type=MESH)

    @pl.loop(0, n_half)
    def _(step):
        peer = {"mp": 2 * step + 1 - core, "dp": dp}
        pl.semaphore_signal(barrier, inc=1, device_id=peer, device_id_type=MESH)

    label_lane = lax.broadcasted_iota(jnp.int32, (SUBLANES, every), 1)
    own_labels = jnp.zeros((SUBLANES, every), jnp.int32)
    for index in range(images):
        own_labels = jnp.where(label_lane == dp * images + index, labels_ref[index], own_labels)
    lab_out[...] = own_labels

    half_gain = gain_ref[...] * math.sqrt(0.5)

    def norm_group(index):
        get_group(index).wait()
        flat = tokens[index * group : (index + 1) * group].astype(F32)
        return layer_norm(flat.reshape(group * tok_count, width), half_gain).astype(BF16)

    n_group = images // group
    normed = norm_group(0)
    get_win.wait()
    for index in range(n_group):
        later = norm_group(index + 1) if index + 1 < n_group else None
        pre = jnp.dot(normed, win[...], preferred_element_type=F32)
        hidden = pre + pre * lax.erf(pre)
        hidden = hidden.reshape(group, tok_count, pre.shape[1])
        hid_sum[index * group : (index + 1) * group, :] = jnp.sum(hidden, axis=1)
        normed = later

    pl.semaphore_wait(barrier, n_chip - 1 + n_half)

    def label_copy(step):
        peer = lax.rem(dp + step, n_dp)
        return pltpu.make_async_remote_copy(
            src_ref=lab_out, dst_ref=labs.at[dp], send_sem=send_sem.at[0], recv_sem=lab_sem,
            device_id={"mp": mp, "dp": peer}, device_id_type=MESH,
        )

    def part_copy(step):
        peer = lax.rem(mp + step, n_mp)
        return pltpu.make_async_remote_copy(
            src_ref=part, dst_ref=part_in.at[mp], send_sem=send_sem.at[1], recv_sem=part_sem,
            device_id={"mp": peer, "dp": dp}, device_id_type=MESH,
        )

    def unit_copy(step):
        peer = lax.rem(dp + step, n_dp)
        return pltpu.make_async_remote_copy(
            src_ref=rows_all.at[core], dst_ref=units.at[core, dp],
            send_sem=send_sem.at[2], recv_sem=unit_sem,
            device_id={"mp": mp, "dp": peer}, device_id_type=MESH,
        )

    def unit_pass():
        return pltpu.make_async_remote_copy(
            src_ref=units.at[core], dst_ref=units.at[core],
            send_sem=send_sem.at[3], recv_sem=fwd_sem,
            device_id=sibling, device_id_type=MESH,
        )

    def stat_swap():
        return pltpu.make_async_remote_copy(
            src_ref=stat_own, dst_ref=stat_pair, send_sem=send_sem.at[4], recv_sem=stat_pair_sem,
            device_id=sibling, device_id_type=MESH,
        )

    def stat_copy(step):
        return pltpu.make_async_remote_copy(
            src_ref=stat_out, dst_ref=stat_in.at[chip], send_sem=send_sem.at[5], recv_sem=stat_sem,
            device_id=at_chip(lax.rem(chip + step, n_chip)), device_id_type=MESH,
        )

    def pick_swap():
        return pltpu.make_async_remote_copy(
            src_ref=pick_pass, dst_ref=pick_pair, send_sem=send_sem.at[6], recv_sem=pick_pair_sem,
            device_id=sibling, device_id_type=MESH,
        )

    def pick_copy(to):
        return pltpu.make_async_remote_copy(
            src_ref=pick_out.at[to // n_dp, lax.rem(to, n_dp)], dst_ref=pick_in.at[chip],
            send_sem=send_sem.at[7], recv_sem=pick_sem,
            device_id=at_chip(to), device_id_type=MESH,
        )

    def grad_swap(to):
        return pltpu.make_async_remote_copy(
            src_ref=grad_pass.at[to], dst_ref=grad_pair.at[to],
            send_sem=send_sem.at[8], recv_sem=grad_pair_sem.at[to],
            device_id=sibling, device_id_type=MESH,
        )

    def grad_copy(to):
        return pltpu.make_async_remote_copy(
            src_ref=grad_out.at[to // n_dp, lax.rem(to, n_dp)], dst_ref=grad_in.at[chip],
            send_sem=send_sem.at[9], recv_sem=grad_sem,
            device_id=at_chip(to), device_id_type=MESH,
        )

    def wait_bytes(ref, count, sem):
        pltpu.make_async_copy(ref.at[pl.ds(0, count)], ref.at[pl.ds(0, count)], sem).wait()

    get_wout.wait()
    hid_mean = hid_sum[...] * (math.sqrt(0.5) / tok_count)
    high = hid_mean.astype(BF16)
    low = (hid_mean - high.astype(F32)).astype(BF16)
    both = jnp.dot(jnp.concatenate([high, low], axis=0), wout[...], preferred_element_type=F32)
    own_part = (both[0:images] + both[images:]).astype(BF16)
    part[...] = own_part

    @pl.loop(1, n_mp)
    def _(step):
        part_copy(lax.rem(step + 1, n_mp - 1) + 1).start()

    @pl.loop(1, n_dp)
    def _(step):
        label_copy(step).start()

    part_in[mp] = own_part
    labs[dp] = own_labels

    @pl.loop(0, n_group)
    def _(index):
        here = pl.ds(pl.multiple_of(index * group, group), group)
        tok_sum[here, :] = jnp.sum(tokens[here].astype(F32), axis=1)

    ones = jnp.ones((128, 128), BF16)

    def scale_chunk(index, carry):
        get_chunk(index).wait()
        here = pl.ds(pl.multiple_of(index * chunk, chunk), chunk)
        squares = None
        for start in range(0, width, 128):
            piece = centres[here, start : start + 128].astype(F32)
            squares = piece * piece if squares is None else squares + piece * piece
        high = squares.astype(BF16)
        low = (squares - high.astype(F32)).astype(BF16)
        total = jnp.dot(high, ones, preferred_element_type=F32)
        total = total + jnp.dot(low, ones, preferred_element_type=F32)
        scales[here, :] = lax.rsqrt(total + 1e-06) * log_scale
        return carry

    lax.fori_loop(0, n_chunk // 2, scale_chunk, 0)

    wait_bytes(part_in, n_mp - 1, part_sem)
    pooled = tok_sum[...] * (1.0 / tok_count) + jnp.sum(part_in[...].astype(F32), axis=0)
    embedding = layer_norm(pooled, final_ref[...])
    length = jnp.sqrt(jnp.sum(embedding * embedding, axis=1, keepdims=True) + 1e-06)
    own_rows = (embedding / length).astype(BF16)
    rows_all[0] = own_rows[:, 0:half]
    rows_all[1] = own_rows[:, half:]

    @pl.loop(0, n_dp)
    def _(step):
        hop = lax.rem(n_dp // 2 + step, n_dp)

        @pl.when(hop != 0)
        def _():
            unit_copy(hop).start()

    units[core, dp] = rows_all[core]
    lax.fori_loop(n_chunk // 2, n_chunk, scale_chunk, 0)

    wait_bytes(labs, n_dp - 1, lab_sem)
    label_row = jnp.sum(labs[...], axis=0)[0:1, :] - offset
    label_col = jnp.broadcast_to(label_row.astype(F32), (128, every)).T[:, 0:1].astype(jnp.int32)
    picked_rows[...] = jnp.zeros_like(picked_rows)

    def pick_chunk(index, carry):
        here = pl.ds(pl.multiple_of(index * chunk, chunk), chunk)
        lane = lax.broadcasted_iota(jnp.int32, (every, chunk), 1)
        picked = jnp.where(lane == label_col - index * chunk, 1.0, 0.0).astype(BF16)
        picked_rows[...] += jnp.dot(picked, centres[here, :], preferred_element_type=F32)
        return carry

    lax.fori_loop(0, n_chunk, pick_chunk, 0)
    own_square = jnp.sum(picked_rows[...] * picked_rows[...], axis=1, keepdims=True)
    own_scale = lax.rsqrt(own_square + 1e-06)

    def pick_block(to_mp):
        here = pl.ds(pl.multiple_of(to_mp * cols, cols), cols)
        return (picked_rows[:, here] * own_scale).astype(BF16).reshape(n_dp, images, cols)

    for to in range(n_half):
        pick_pass[to] = pick_block(2 * to + 1 - core)
    pick_swap().start()

    wait_bytes(units.at[core], n_dp - 1, unit_sem)
    unit_pass().start()

    def place_units(index):
        here = pl.ds(pl.multiple_of(index * half, half), half)
        rows = units[index].reshape(every, half)
        unit_full[:, here] = rows
        unit_t[here, :] = rows.T

    def half_dot(here, index):
        part_of = pl.ds(pl.multiple_of(index * half, half), half)
        return jnp.dot(centres[here, part_of], unit_t[part_of, :], preferred_element_type=F32)

    place_units(core)
    early = raw_half.shape[0]
    raw_half[...] = half_dot(pl.ds(0, early), core)

    pick_swap().wait_recv()
    for to in range(n_half):
        pick_out[to] = pick_block(2 * to + core) + pick_pair[to]

    @pl.loop(1, n_chip)
    def _(step):
        pick_copy(lax.rem(chip + step, n_chip)).start()

    pick_in[chip] = pick_out[side, dp]
    unit_pass().wait_recv()
    place_units(1 - core)

    def weigh(start, count, raw, carry):
        total, inner = carry
        here = pl.ds(start, count)
        scale = scales[here, :]
        if every > 128:
            scale = jnp.concatenate([scale] * (every // 128), axis=1)
        picked = lax.broadcasted_iota(jnp.int32, (count, every), 0) == label_row - start
        exponent = jnp.where(picked, 0.0, jnp.exp2(raw * scale))
        weight = (exponent * scale).astype(BF16)
        weights[:, here] = weight.T
        return (
            total + fold_rows(exponent),
            inner + fold_rows(weight.astype(F32) * raw),
        )

    def class_chunk(index, carry):
        start = early + index * wide
        if not isinstance(start, int):
            start = pl.multiple_of(start, 128)
        raw = jnp.dot(centres[pl.ds(start, wide), :], unit_t[...], preferred_element_type=F32)
        return weigh(start, wide, raw, carry)

    zeros = jnp.zeros((SUBLANES, every), F32)
    raw = raw_half[...] + half_dot(pl.ds(0, early), 1 - core)
    sums = weigh(0, early, raw, (zeros, zeros))
    wide = 3 * early // 2
    n_wide = (classes - early) // wide
    if n_wide <= 2:
        for index in range(n_wide):
            sums = class_chunk(index, sums)
    else:
        sums = lax.fori_loop(0, n_wide, class_chunk, sums)
    total, inner = sums
    target = jnp.zeros((every, 128), F32)
    for start in range(0, width, 128):
        picked = (picked_rows[:, start : start + 128] * own_scale).astype(BF16).astype(F32)
        target = target + unit_full[:, start : start + 128].astype(F32) * picked
    stat_own[0:1, :] = jnp.sum(total, axis=0, keepdims=True)
    stat_own[1:2, :] = jnp.sum(inner, axis=0, keepdims=True)
    stat_own[2:3, :] = jnp.sum(target.T, axis=0, keepdims=True)
    stat_own[3:4, :] = jnp.zeros((1, every), F32)
    stat_swap().start()

    def grad_block(to_mp):
        here = pl.ds(pl.multiple_of(to_mp * cols, cols), cols)
        return jnp.dot(weights[...], centres[:, here], preferred_element_type=F32)

    def pass_cols(step, carry):
        to = lax.rem(side + 1 + step, n_half)
        grad_pass[to] = grad_block(2 * to + 1 - core).astype(BF16).reshape(n_dp, images, cols)
        grad_swap(to).start()
        return carry

    lax.fori_loop(0, n_half, pass_cols, 0)
    stat_swap().wait_recv()
    chip_stats = stat_own[...] + stat_pair[...]
    stat_out[...] = chip_stats

    @pl.loop(1, n_chip)
    def _(step):
        stat_copy(step).start()

    stat_in[chip] = chip_stats

    def send_cols(step, carry):
        to = lax.rem(side + 1 + step, n_half)
        grad_swap(to).wait_recv()
        block = grad_block(2 * to + core) + grad_pair[to].reshape(every, cols).astype(F32)
        grad_out[to] = block.astype(BF16).reshape(n_dp, images, cols)

        @pl.loop(0, n_dp)
        def _(hop):
            peer = to * n_dp + lax.rem(dp + n_dp // 2 + hop, n_dp)

            @pl.when(peer != chip)
            def _():
                grad_copy(peer).start()

        return carry

    lax.fori_loop(0, n_half, send_cols, 0)
    grad_in[chip] = grad_out[side, dp]

    wait_bytes(stat_in, n_chip - 1, stat_sem)
    stat_sum[...] = jnp.zeros_like(stat_sum)
    stat_sum[0:STATS, :] = jnp.sum(stat_in[...], axis=0)
    picked_rows[:, 0:128] = stat_sum[...].T
    stats = picked_rows[pl.ds(pl.multiple_of(dp * images, images), images), 0:128]
    others, inner_sum, target_cos = stats[:, 0:1], stats[:, 1:2], stats[:, 2:3]
    shifted, slope = arc_target(target_cos)
    target_exp = jnp.exp(logit_scale * shifted)
    totals = others + target_exp
    rate = logit_scale / totals
    target_weight = (logit_scale * ((target_exp / totals - 1.0) * slope)).astype(BF16).astype(F32)
    rate = rate * (1.0 / log_scale)
    inner_all = rate * inner_sum + target_weight * target_cos
    diagonal = lax.broadcasted_iota(jnp.int32, (images, images), 0) == lax.broadcasted_iota(
        jnp.int32, (images, images), 1
    )
    row_loss = jnp.log(totals) - logit_scale * shifted
    loss_ref[...] = jnp.sum(jnp.where(diagonal, row_loss, 0.0), axis=0, keepdims=True)
    unit_here = unit_full[
        pl.ds(pl.multiple_of(dp * images, images), images),
        pl.ds(pl.multiple_of(mp * cols, cols), cols),
    ].astype(F32)
    wait_bytes(pick_in, n_chip - 1, pick_sem)
    centre_rows = jnp.sum(pick_in[...].astype(F32), axis=0)
    rest = target_weight * centre_rows - unit_here * inner_all
    wait_bytes(grad_in, n_chip - 1, grad_sem)
    gathered = jnp.sum(grad_in[...].astype(F32), axis=0)
    grad_ref[...] = (gathered * rate + rest) / length

    @pl.loop(1, n_mp)
    def _(step):
        part_copy(step).wait_send()

    @pl.loop(1, n_dp)
    def _(step):
        label_copy(step).wait_send()
        unit_copy(step).wait_send()

    unit_pass().wait_send()
    stat_swap().wait_send()
    pick_swap().wait_send()

    @pl.loop(0, n_half)
    def _(to):
        grad_swap(to).wait_send()

    @pl.loop(1, n_chip)
    def _(step):
        peer = lax.rem(chip + step, n_chip)
        stat_copy(step).wait_send()
        pick_copy(peer).wait_send()
        grad_copy(peer).wait_send()


def shards(n_mp, n_dp, tokens, norm_gain, weight_in, weight_out, final_gain, centres, labels):
    images, tok_count, width = tokens.shape
    hidden = weight_in.shape[1]
    classes = centres.shape[0]
    every = images * n_dp
    n_half = n_mp // 2
    n_chip = n_half * n_dp
    cols = width // n_mp
    chunk = min(1024, classes)
    group = 8
    any_spec = pl.BlockSpec(memory_space=pltpu.HBM)
    vmem_spec = pl.BlockSpec(memory_space=pltpu.VMEM)
    loss, grad = pl.pallas_call(
        functools.partial(kernel, n_mp, n_dp, chunk, group),
        out_shape=(
            jax.ShapeDtypeStruct((1, images), F32),
            jax.ShapeDtypeStruct((images, cols), F32),
        ),
        in_specs=[any_spec, vmem_spec, any_spec, any_spec, vmem_spec, any_spec,
            pl.BlockSpec(memory_space=pltpu.SMEM)],
        out_specs=(vmem_spec, vmem_spec),
        scratch_shapes=[
            pltpu.VMEM((images, tok_count, width), BF16),
            pltpu.VMEM((width, hidden), BF16),
            pltpu.VMEM((hidden, width), BF16),
            pltpu.VMEM((classes, width), BF16),
            pltpu.VMEM((n_dp, SUBLANES, every), jnp.int32),
            pltpu.VMEM((images, hidden), F32),
            pltpu.VMEM((images, width), F32),
            pltpu.VMEM((images, width), BF16),
            pltpu.VMEM((n_mp, images, width), BF16),
            pltpu.VMEM((2, n_dp, images, width // 2), BF16),
            pltpu.VMEM((every, width), BF16),
            pltpu.VMEM((width, every), BF16),
            pltpu.VMEM((classes // 4 * 128 // every, every), F32),
            pltpu.VMEM((2, images, width // 2), BF16),
            pltpu.VMEM((classes, 128), F32),
            pltpu.VMEM((every, width), F32),
            pltpu.VMEM((every, classes), BF16),
            pltpu.VMEM((STATS, every), F32),
            pltpu.VMEM((STATS, every), F32),
            pltpu.VMEM((STATS, every), F32),
            pltpu.VMEM((n_chip, STATS, every), F32),
            pltpu.VMEM((128, every), F32),
            pltpu.VMEM((n_half, n_dp, images, cols), BF16),
            pltpu.VMEM((n_half, n_dp, images, cols), BF16),
            pltpu.VMEM((n_half, n_dp, images, cols), BF16),
            pltpu.VMEM((n_chip, images, cols), BF16),
            pltpu.VMEM((n_half, n_dp, images, cols), BF16),
            pltpu.VMEM((n_half, n_dp, images, cols), BF16),
            pltpu.VMEM((n_half, n_dp, images, cols), BF16),
            pltpu.VMEM((n_chip, images, cols), BF16),
            pltpu.VMEM((SUBLANES, every), jnp.int32),
            pltpu.SemaphoreType.DMA((images // group,)),
            pltpu.SemaphoreType.DMA((2,)),
            pltpu.SemaphoreType.DMA((classes // chunk,)),
            pltpu.SemaphoreType.DMA((10,)),
            pltpu.SemaphoreType.DMA,
            pltpu.SemaphoreType.DMA,
            pltpu.SemaphoreType.DMA,
            pltpu.SemaphoreType.DMA,
            pltpu.SemaphoreType.DMA,
            pltpu.SemaphoreType.DMA,
            pltpu.SemaphoreType.DMA,
            pltpu.SemaphoreType.DMA,
            pltpu.SemaphoreType.DMA((n_half,)),
            pltpu.SemaphoreType.DMA,
        ],
        compiler_params=pltpu.CompilerParams(
            collective_id=0, has_side_effects=True, vmem_limit_bytes=56 * 1024 * 1024
        ),
    )(
        tokens, norm_gain.reshape(1, width), weight_in, weight_out,
        final_gain.reshape(1, width), centres, labels,
    )
    def emit(loss_in, grad_in, loss_out, grad_out):
        loss_out[...] = loss_in[...]
        grad_out[...] = grad_in[...]

    loss, grad = pl.pallas_call(
        emit,
        out_shape=(
            jax.ShapeDtypeStruct((1, images), F32),
            jax.ShapeDtypeStruct((images, cols), F32),
        ),
        in_specs=[vmem_spec, vmem_spec],
        out_specs=(vmem_spec, vmem_spec),
    )(loss, grad)
    return (loss.reshape(images), grad)


def solution(mesh):
    return jax.shard_map(
        functools.partial(shards, mesh.shape["mp"], mesh.shape["dp"]),
        mesh=mesh,
        in_specs=(
            P("dp", None, None),
            P(),
            P(None, "mp"),
            P("mp", None),
            P(),
            P(("mp", "dp"), None),
            P("dp"),
        ),
        out_specs=(P("dp"), P("dp", "mp")),
        check_vma=False,
    )
```

```python
import functools
import math

import jax
import jax.numpy as jnp
from jax import lax
from jax.experimental import pallas as pl
from jax.experimental.pallas import tpu as pltpu
from jax.sharding import PartitionSpec as P

logit_scale = 64.0
angle_margin = 0.5
MESH = pl.DeviceIdType.MESH
F32 = jnp.float32
BF16 = jnp.bfloat16
STATS = 4
SUBLANES = 8


def layer_norm(values, gain_vec):
    average = jnp.mean(values, axis=-1, keepdims=True)
    centred = values - average
    variance = jnp.mean(centred * centred, axis=-1, keepdims=True)
    return centred * lax.rsqrt(variance + 1e-06) * gain_vec


def arc_target(target_cos):
    target_sine = jnp.sqrt(jnp.maximum(1.0 - target_cos * target_cos, 0.01))
    inside = target_cos > -math.cos(angle_margin)
    shifted = jnp.where(
        inside,
        target_cos * math.cos(angle_margin) - target_sine * math.sin(angle_margin),
        target_cos - angle_margin * math.sin(angle_margin),
    )
    margin_slope = jnp.where(
        inside, math.cos(angle_margin) + math.sin(angle_margin) * target_cos / target_sine, 1.0
    )
    return (shifted, margin_slope)


def fold_rows(values):
    return jnp.sum(values.reshape(-1, SUBLANES, values.shape[1]), axis=0)


def nt_dot(left, right):
    return lax.dot_general(left, right, (((1,), (1,)), ((), ())), preferred_element_type=F32)


def kernel(
    n_mp, n_dp, chunk, group,
    tokens_hbm, gain_ref, win_hbm, wout_hbm, final_ref, centres_hbm, labels_ref,
    loss_ref, grad_ref,
    tokens, win, wout, centres, labs, hid_sum, tok_sum, part, part_in, units, unit_full, unit_t, raw_half, rows_all,
    scales, picked_rows, weights, stat_own, stat_pair, stat_out, stat_in, stat_sum,
    pick_pass, pick_pair, pick_out, pick_in, grad_pass, grad_pair, grad_out, grad_in, lab_out,
    tok_sem, w_sem, c_sem, send_sem, lab_sem, part_sem, unit_sem, fwd_sem, stat_pair_sem, stat_sem,
    pick_pair_sem, pick_sem, grad_pair_sem, grad_sem,
):
    n_half = n_mp // 2
    n_chip = n_half * n_dp
    mp, dp = lax.axis_index("mp"), lax.axis_index("dp")
    me = mp * n_dp + dp
    core, side = lax.rem(mp, 2), mp // 2
    chip = side * n_dp + dp
    sibling = {"mp": mp + 1 - 2 * core, "dp": dp}
    images, tok_count, width = tokens.shape
    every = images * n_dp
    classes = centres.shape[0]
    n_chunk = classes // chunk
    cols = width // n_mp
    half = width // 2
    offset = me * classes
    log_scale = logit_scale * math.log2(math.e)

    def at_chip(index):
        return {"mp": 2 * (index // n_dp) + core, "dp": lax.rem(index, n_dp)}

    def get_group(index):
        return pltpu.make_async_copy(
            tokens_hbm.at[pl.ds(index * group, group)],
            tokens.at[pl.ds(index * group, group)],
            tok_sem.at[index],
        )

    def get_chunk(index):
        here = pl.ds(pl.multiple_of(index * chunk, chunk), chunk)
        return pltpu.make_async_copy(centres_hbm.at[here], centres.at[here], c_sem.at[index])

    get_win = pltpu.make_async_copy(win_hbm, win, w_sem.at[0])
    get_wout = pltpu.make_async_copy(wout_hbm, wout, w_sem.at[1])
    get_group(0).start()
    get_win.start()
    for index in range(1, images // group):
        get_group(index).start()
    get_wout.start()

    @pl.loop(0, n_chunk)
    def _(index):
        get_chunk(index).start()

    barrier = pltpu.get_barrier_semaphore()

    @pl.loop(1, n_chip)
    def _(step):
        peer = at_chip(lax.rem(chip + step, n_chip))
        pl.semaphore_signal(barrier, inc=1, device_id=peer, device_id_type=MESH)

    @pl.loop(0, n_half)
    def _(step):
        peer = {"mp": 2 * step + 1 - core, "dp": dp}
        pl.semaphore_signal(barrier, inc=1, device_id=peer, device_id_type=MESH)

    label_lane = lax.broadcasted_iota(jnp.int32, (SUBLANES, every), 1)
    own_labels = jnp.zeros((SUBLANES, every), jnp.int32)
    for index in range(images):
        own_labels = jnp.where(label_lane == dp * images + index, labels_ref[index], own_labels)
    lab_out[...] = own_labels

    half_gain = gain_ref[...] * math.sqrt(0.5)

    def norm_group(index):
        get_group(index).wait()
        flat = tokens[index * group : (index + 1) * group].astype(F32)
        return layer_norm(flat.reshape(group * tok_count, width), half_gain).astype(BF16)

    n_group = images // group
    normed = norm_group(0)
    get_win.wait()
    pl.semaphore_wait(barrier, n_chip - 1 + n_half)

    def label_copy(step):
        peer = lax.rem(dp + step, n_dp)
        return pltpu.make_async_remote_copy(
            src_ref=lab_out, dst_ref=labs.at[dp], send_sem=send_sem.at[0], recv_sem=lab_sem,
            device_id={"mp": mp, "dp": peer}, device_id_type=MESH,
        )

    @pl.loop(1, n_dp)
    def _(step):
        label_copy(step).start()

    labs[dp] = own_labels

    for index in range(n_group):
        later = norm_group(index + 1) if index + 1 < n_group else None
        pre = jnp.dot(normed, win[...], preferred_element_type=F32)
        hidden = pre + pre * lax.erf(pre)
        hidden = hidden.reshape(group, tok_count, pre.shape[1])
        hid_sum[index * group : (index + 1) * group, :] = jnp.sum(hidden, axis=1)
        normed = later


    def part_copy(step):
        peer = lax.rem(mp + step, n_mp)
        return pltpu.make_async_remote_copy(
            src_ref=part, dst_ref=part_in.at[mp], send_sem=send_sem.at[1], recv_sem=part_sem,
            device_id={"mp": peer, "dp": dp}, device_id_type=MESH,
        )

    def unit_copy(step):
        peer = lax.rem(dp + step, n_dp)
        return pltpu.make_async_remote_copy(
            src_ref=rows_all.at[core], dst_ref=units.at[core, dp],
            send_sem=send_sem.at[2], recv_sem=unit_sem,
            device_id={"mp": mp, "dp": peer}, device_id_type=MESH,
        )

    def unit_pass():
        return pltpu.make_async_remote_copy(
            src_ref=units.at[core], dst_ref=units.at[core],
            send_sem=send_sem.at[3], recv_sem=fwd_sem,
            device_id=sibling, device_id_type=MESH,
        )

    def stat_swap():
        return pltpu.make_async_remote_copy(
            src_ref=stat_own, dst_ref=stat_pair, send_sem=send_sem.at[4], recv_sem=stat_pair_sem,
            device_id=sibling, device_id_type=MESH,
        )

    def stat_copy(step):
        return pltpu.make_async_remote_copy(
            src_ref=stat_out, dst_ref=stat_in.at[chip], send_sem=send_sem.at[5], recv_sem=stat_sem,
            device_id=at_chip(lax.rem(chip + step, n_chip)), device_id_type=MESH,
        )

    def pick_swap():
        return pltpu.make_async_remote_copy(
            src_ref=pick_pass, dst_ref=pick_pair, send_sem=send_sem.at[6], recv_sem=pick_pair_sem,
            device_id=sibling, device_id_type=MESH,
        )

    def pick_copy(to):
        return pltpu.make_async_remote_copy(
            src_ref=pick_out.at[to // n_dp, lax.rem(to, n_dp)], dst_ref=pick_in.at[chip],
            send_sem=send_sem.at[7], recv_sem=pick_sem,
            device_id=at_chip(to), device_id_type=MESH,
        )

    def grad_swap(to):
        return pltpu.make_async_remote_copy(
            src_ref=grad_pass.at[to], dst_ref=grad_pair.at[to],
            send_sem=send_sem.at[8], recv_sem=grad_pair_sem.at[to],
            device_id=sibling, device_id_type=MESH,
        )

    def grad_copy(to):
        return pltpu.make_async_remote_copy(
            src_ref=grad_out.at[to // n_dp, lax.rem(to, n_dp)], dst_ref=grad_in.at[chip],
            send_sem=send_sem.at[9], recv_sem=grad_sem,
            device_id=at_chip(to), device_id_type=MESH,
        )

    def wait_bytes(ref, count, sem):
        pltpu.make_async_copy(ref.at[pl.ds(0, count)], ref.at[pl.ds(0, count)], sem).wait()

    get_wout.wait()
    hid_mean = hid_sum[...] * (math.sqrt(0.5) / tok_count)
    high = hid_mean.astype(BF16)
    low = (hid_mean - high.astype(F32)).astype(BF16)
    both = jnp.dot(jnp.concatenate([high, low], axis=0), wout[...], preferred_element_type=F32)
    own_part = (both[0:images] + both[images:]).astype(BF16)
    part[...] = own_part

    @pl.loop(1, n_mp)
    def _(step):
        part_copy(lax.rem(step + 1, n_mp - 1) + 1).start()

    part_in[mp] = own_part

    @pl.loop(0, n_group)
    def _(index):
        here = pl.ds(pl.multiple_of(index * group, group), group)
        tok_sum[here, :] = jnp.sum(tokens[here].astype(F32), axis=1)

    ones = jnp.ones((128, 128), BF16)

    def scale_chunk(index, carry):
        get_chunk(index).wait()
        here = pl.ds(pl.multiple_of(index * chunk, chunk), chunk)
        squares = None
        for start in range(0, width, 128):
            piece = centres[here, start : start + 128].astype(F32)
            squares = piece * piece if squares is None else squares + piece * piece
        high = squares.astype(BF16)
        low = (squares - high.astype(F32)).astype(BF16)
        total = jnp.dot(high, ones, preferred_element_type=F32)
        total = total + jnp.dot(low, ones, preferred_element_type=F32)
        scales[here, :] = lax.rsqrt(total + 1e-06) * log_scale
        return carry

    n_first = n_chunk // 2
    lax.fori_loop(0, n_first, scale_chunk, 0)

    wait_bytes(part_in, n_mp - 1, part_sem)
    pooled = tok_sum[...] * (1.0 / tok_count) + jnp.sum(part_in[...].astype(F32), axis=0)
    embedding = layer_norm(pooled, final_ref[...])
    length = jnp.sqrt(jnp.sum(embedding * embedding, axis=1, keepdims=True) + 1e-06)
    own_rows = (embedding / length).astype(BF16)
    rows_all[0] = own_rows[:, 0:half]
    rows_all[1] = own_rows[:, half:]

    @pl.loop(0, n_dp)
    def _(step):
        hop = lax.rem(n_dp // 2 + step, n_dp)

        @pl.when(hop != 0)
        def _():
            unit_copy(hop).start()

    units[core, dp] = rows_all[core]

    wait_bytes(labs, n_dp - 1, lab_sem)
    label_row = jnp.sum(labs[...], axis=0)[0:1, :] - offset
    label_col = jnp.broadcast_to(label_row.astype(F32), (128, every)).T[:, 0:1].astype(jnp.int32)
    picked_rows[...] = jnp.zeros_like(picked_rows)

    def pick_dot(index):
        here = pl.ds(pl.multiple_of(index * chunk, chunk), chunk)
        lane = lax.broadcasted_iota(jnp.int32, (every, chunk), 1)
        picked = jnp.where(lane == label_col - index * chunk, 1.0, 0.0).astype(BF16)
        return jnp.dot(picked, centres[here, :], preferred_element_type=F32)

    def scale_and_pick(index, carry):
        carry = scale_chunk(index, carry)
        first = pick_dot(index - n_first)
        picked_rows[...] += first + pick_dot(index)
        return carry

    lax.fori_loop(n_first, n_chunk, scale_and_pick, 0)
    own_square = jnp.sum(picked_rows[...] * picked_rows[...], axis=1, keepdims=True)
    own_scale = lax.rsqrt(own_square + 1e-06)

    def pick_block(to_mp):
        here = pl.ds(pl.multiple_of(to_mp * cols, cols), cols)
        return (picked_rows[:, here] * own_scale).astype(BF16).reshape(n_dp, images, cols)

    for to in range(n_half):
        pick_pass[to] = pick_block(2 * to + 1 - core)
    pick_swap().start()

    wait_bytes(units.at[core], n_dp - 1, unit_sem)
    unit_pass().start()

    def place_units(index):
        here = pl.ds(pl.multiple_of(index * half, half), half)
        rows = units[index].reshape(every, half)
        unit_full[:, here] = rows
        unit_t[here, :] = rows.T

    def half_dot(here, index):
        part_of = pl.ds(pl.multiple_of(index * half, half), half)
        return jnp.dot(centres[here, part_of], unit_t[part_of, :], preferred_element_type=F32)

    place_units(core)
    early = raw_half.shape[0]
    raw_half[...] = half_dot(pl.ds(0, early), core)

    pick_swap().wait_recv()
    for to in range(n_half):
        pick_out[to] = pick_block(2 * to + core) + pick_pair[to]

    @pl.loop(1, n_chip)
    def _(step):
        pick_copy(lax.rem(chip + step, n_chip)).start()

    pick_in[chip] = pick_out[side, dp]
    unit_pass().wait_recv()
    place_units(1 - core)

    def weigh(start, count, raw, carry):
        total, inner = carry
        here = pl.ds(start, count)
        scale = scales[here, :]
        if every > 128:
            scale = jnp.concatenate([scale] * (every // 128), axis=1)
        picked = lax.broadcasted_iota(jnp.int32, (count, every), 0) == label_row - start
        exponent = jnp.where(picked, 0.0, jnp.exp2(raw * scale))
        weight = (exponent * scale).astype(BF16)
        weights[:, here] = weight.T
        return (
            total + fold_rows(exponent),
            inner + fold_rows(weight.astype(F32) * raw),
        )

    def class_chunk(index, carry):
        start = early + index * wide
        if not isinstance(start, int):
            start = pl.multiple_of(start, 128)
        raw = jnp.dot(centres[pl.ds(start, wide), :], unit_t[...], preferred_element_type=F32)
        return weigh(start, wide, raw, carry)

    zeros = jnp.zeros((SUBLANES, every), F32)
    raw = raw_half[...] + half_dot(pl.ds(0, early), 1 - core)
    sums = weigh(0, early, raw, (zeros, zeros))
    wide = 3 * early // 2
    n_wide = (classes - early) // wide
    if n_wide <= 2:
        for index in range(n_wide):
            sums = class_chunk(index, sums)
    else:
        sums = lax.fori_loop(0, n_wide, class_chunk, sums)
    total, inner = sums
    target = jnp.zeros((every, 128), F32)
    for start in range(0, width, 128):
        picked = (picked_rows[:, start : start + 128] * own_scale).astype(BF16).astype(F32)
        target = target + unit_full[:, start : start + 128].astype(F32) * picked
    stat_own[0:1, :] = jnp.sum(total, axis=0, keepdims=True)
    stat_own[1:2, :] = jnp.sum(inner, axis=0, keepdims=True)
    stat_own[2:3, :] = jnp.sum(target.T, axis=0, keepdims=True)
    stat_own[3:4, :] = jnp.zeros((1, every), F32)
    stat_swap().start()

    def grad_block(to_mp):
        here = pl.ds(pl.multiple_of(to_mp * cols, cols), cols)
        return jnp.dot(weights[...], centres[:, here], preferred_element_type=F32)

    def pass_cols(step, carry):
        to = lax.rem(side + 1 + step, n_half)
        grad_pass[to] = grad_block(2 * to + 1 - core).astype(BF16).reshape(n_dp, images, cols)
        grad_swap(to).start()
        return carry

    lax.fori_loop(0, n_half, pass_cols, 0)
    stat_swap().wait_recv()
    chip_stats = stat_own[...] + stat_pair[...]
    stat_out[...] = chip_stats

    @pl.loop(1, n_chip)
    def _(step):
        stat_copy(step).start()

    stat_in[chip] = chip_stats

    def send_cols(step, carry):
        to = lax.rem(side + 1 + step, n_half)
        grad_swap(to).wait_recv()
        block = grad_block(2 * to + core) + grad_pair[to].reshape(every, cols).astype(F32)
        grad_out[to] = block.astype(BF16).reshape(n_dp, images, cols)

        @pl.loop(0, n_dp)
        def _(hop):
            peer = to * n_dp + lax.rem(dp + n_dp // 2 + hop, n_dp)

            @pl.when(peer != chip)
            def _():
                grad_copy(peer).start()

        return carry

    lax.fori_loop(0, n_half, send_cols, 0)
    grad_in[chip] = grad_out[side, dp]

    @pl.loop(1, n_mp)
    def _(step):
        part_copy(step).wait_send()

    @pl.loop(1, n_dp)
    def _(step):
        label_copy(step).wait_send()
        unit_copy(step).wait_send()

    unit_pass().wait_send()
    stat_swap().wait_send()
    pick_swap().wait_send()

    @pl.loop(0, n_half)
    def _(to):
        grad_swap(to).wait_send()

    @pl.loop(1, n_chip)
    def _(step):
        stat_copy(step).wait_send()
        pick_copy(lax.rem(chip + step, n_chip)).wait_send()

    wait_bytes(stat_in, n_chip - 1, stat_sem)
    stat_sum[...] = jnp.zeros_like(stat_sum)
    stat_sum[0:STATS, :] = jnp.sum(stat_in[...], axis=0)
    picked_rows[:, 0:128] = stat_sum[...].T
    stats = picked_rows[pl.ds(pl.multiple_of(dp * images, images), images), 0:128]
    others, inner_sum, target_cos = stats[:, 0:1], stats[:, 1:2], stats[:, 2:3]
    shifted, slope = arc_target(target_cos)
    target_exp = jnp.exp(logit_scale * shifted)
    totals = others + target_exp
    rate = logit_scale / totals
    target_weight = (logit_scale * ((target_exp / totals - 1.0) * slope)).astype(BF16).astype(F32)
    rate = rate * (1.0 / log_scale)
    inner_all = rate * inner_sum + target_weight * target_cos
    diagonal = lax.broadcasted_iota(jnp.int32, (images, images), 0) == lax.broadcasted_iota(
        jnp.int32, (images, images), 1
    )
    row_loss = jnp.log(totals) - logit_scale * shifted
    loss_ref[...] = jnp.sum(jnp.where(diagonal, row_loss, 0.0), axis=0, keepdims=True)
    unit_here = unit_full[
        pl.ds(pl.multiple_of(dp * images, images), images),
        pl.ds(pl.multiple_of(mp * cols, cols), cols),
    ].astype(F32)
    wait_bytes(pick_in, n_chip - 1, pick_sem)
    centre_rows = jnp.sum(pick_in[...].astype(F32), axis=0)
    rest = target_weight * centre_rows - unit_here * inner_all
    wait_bytes(grad_in, n_chip - 1, grad_sem)
    gathered = jnp.sum(grad_in[...].astype(F32), axis=0)
    grad_ref[...] = (gathered * rate + rest) / length

    @pl.loop(1, n_chip)
    def _(step):
        peer = lax.rem(chip + step, n_chip)
        grad_copy(peer).wait_send()


def shards(n_mp, n_dp, tokens, norm_gain, weight_in, weight_out, final_gain, centres, labels):
    images, tok_count, width = tokens.shape
    hidden = weight_in.shape[1]
    classes = centres.shape[0]
    every = images * n_dp
    n_half = n_mp // 2
    n_chip = n_half * n_dp
    cols = width // n_mp
    chunk = min(1024, classes)
    group = 8
    any_spec = pl.BlockSpec(memory_space=pltpu.HBM)
    vmem_spec = pl.BlockSpec(memory_space=pltpu.VMEM)
    loss, grad = pl.pallas_call(
        functools.partial(kernel, n_mp, n_dp, chunk, group),
        out_shape=(
            jax.ShapeDtypeStruct((1, images), F32),
            jax.ShapeDtypeStruct((images, cols), F32),
        ),
        in_specs=[any_spec, vmem_spec, any_spec, any_spec, vmem_spec, any_spec,
            pl.BlockSpec(memory_space=pltpu.SMEM)],
        out_specs=(vmem_spec, vmem_spec),
        scratch_shapes=[
            pltpu.VMEM((images, tok_count, width), BF16),
            pltpu.VMEM((width, hidden), BF16),
            pltpu.VMEM((hidden, width), BF16),
            pltpu.VMEM((classes, width), BF16),
            pltpu.VMEM((n_dp, SUBLANES, every), jnp.int32),
            pltpu.VMEM((images, hidden), F32),
            pltpu.VMEM((images, width), F32),
            pltpu.VMEM((images, width), BF16),
            pltpu.VMEM((n_mp, images, width), BF16),
            pltpu.VMEM((2, n_dp, images, width // 2), BF16),
            pltpu.VMEM((every, width), BF16),
            pltpu.VMEM((width, every), BF16),
            pltpu.VMEM((classes // 4 * 128 // every, every), F32),
            pltpu.VMEM((2, images, width // 2), BF16),
            pltpu.VMEM((classes, 128), F32),
            pltpu.VMEM((every, width), F32),
            pltpu.VMEM((every, classes), BF16),
            pltpu.VMEM((STATS, every), F32),
            pltpu.VMEM((STATS, every), F32),
            pltpu.VMEM((STATS, every), F32),
            pltpu.VMEM((n_chip, STATS, every), F32),
            pltpu.VMEM((128, every), F32),
            pltpu.VMEM((n_half, n_dp, images, cols), BF16),
            pltpu.VMEM((n_half, n_dp, images, cols), BF16),
            pltpu.VMEM((n_half, n_dp, images, cols), BF16),
            pltpu.VMEM((n_chip, images, cols), BF16),
            pltpu.VMEM((n_half, n_dp, images, cols), BF16),
            pltpu.VMEM((n_half, n_dp, images, cols), BF16),
            pltpu.VMEM((n_half, n_dp, images, cols), BF16),
            pltpu.VMEM((n_chip, images, cols), BF16),
            pltpu.VMEM((SUBLANES, every), jnp.int32),
            pltpu.SemaphoreType.DMA((images // group,)),
            pltpu.SemaphoreType.DMA((2,)),
            pltpu.SemaphoreType.DMA((classes // chunk,)),
            pltpu.SemaphoreType.DMA((10,)),
            pltpu.SemaphoreType.DMA,
            pltpu.SemaphoreType.DMA,
            pltpu.SemaphoreType.DMA,
            pltpu.SemaphoreType.DMA,
            pltpu.SemaphoreType.DMA,
            pltpu.SemaphoreType.DMA,
            pltpu.SemaphoreType.DMA,
            pltpu.SemaphoreType.DMA,
            pltpu.SemaphoreType.DMA((n_half,)),
            pltpu.SemaphoreType.DMA,
        ],
        compiler_params=pltpu.CompilerParams(
            collective_id=0, has_side_effects=True, vmem_limit_bytes=56 * 1024 * 1024
        ),
    )(
        tokens, norm_gain.reshape(1, width), weight_in, weight_out,
        final_gain.reshape(1, width), centres, labels,
    )
    def emit(loss_in, grad_in, loss_out, grad_out):
        loss_out[...] = loss_in[...]
        grad_out[...] = grad_in[...]

    loss, grad = pl.pallas_call(
        emit,
        out_shape=(
            jax.ShapeDtypeStruct((1, images), F32),
            jax.ShapeDtypeStruct((images, cols), F32),
        ),
        in_specs=[vmem_spec, vmem_spec],
        out_specs=(vmem_spec, vmem_spec),
    )(loss, grad)
    return (loss.reshape(images), grad)


def solution(mesh):
    return jax.shard_map(
        functools.partial(shards, mesh.shape["mp"], mesh.shape["dp"]),
        mesh=mesh,
        in_specs=(
            P("dp", None, None),
            P(),
            P(None, "mp"),
            P("mp", None),
            P(),
            P(("mp", "dp"), None),
            P("dp"),
        ),
        out_specs=(P("dp"), P("dp", "mp")),
        check_vma=False,
    )
```

```python
import functools
import math

import jax
import jax.numpy as jnp
from jax import lax
from jax.experimental import pallas as pl
from jax.experimental.pallas import tpu as pltpu
from jax.sharding import PartitionSpec as P

logit_scale = 64.0
angle_margin = 0.5
MESH = pl.DeviceIdType.MESH
F32 = jnp.float32
BF16 = jnp.bfloat16
STATS = 4
SUBLANES = 8


def layer_norm(values, gain_vec):
    average = jnp.mean(values, axis=-1, keepdims=True)
    centred = values - average
    variance = jnp.mean(centred * centred, axis=-1, keepdims=True)
    return centred * lax.rsqrt(variance + 1e-06) * gain_vec


def arc_target(target_cos):
    target_sine = jnp.sqrt(jnp.maximum(1.0 - target_cos * target_cos, 0.01))
    inside = target_cos > -math.cos(angle_margin)
    shifted = jnp.where(
        inside,
        target_cos * math.cos(angle_margin) - target_sine * math.sin(angle_margin),
        target_cos - angle_margin * math.sin(angle_margin),
    )
    margin_slope = jnp.where(
        inside, math.cos(angle_margin) + math.sin(angle_margin) * target_cos / target_sine, 1.0
    )
    return (shifted, margin_slope)


def fold_rows(values):
    return jnp.sum(values.reshape(-1, SUBLANES, values.shape[1]), axis=0)


def nt_dot(left, right):
    return lax.dot_general(left, right, (((1,), (1,)), ((), ())), preferred_element_type=F32)


def kernel(
    n_mp, n_dp, chunk, group,
    tokens_hbm, gain_ref, win_hbm, wout_hbm, final_ref, centres_hbm, labels_ref,
    loss_ref, grad_ref,
    tokens, win, wout, centres, labs, hid_sum, tok_sum, part, part_in, units, unit_full, unit_t, raw_half, rows_all,
    scales, picked_rows, weights, stat_own, stat_pair, stat_out, stat_in, stat_sum,
    pick_pass, pick_pair, pick_out, pick_in, grad_pass, grad_pair, grad_out, grad_in, lab_out,
    tok_sem, w_sem, c_sem, send_sem, lab_sem, part_sem, unit_sem, fwd_sem, stat_pair_sem, stat_sem,
    pick_pair_sem, pick_sem, grad_pair_sem, grad_sem,
):
    n_half = n_mp // 2
    n_chip = n_half * n_dp
    mp, dp = lax.axis_index("mp"), lax.axis_index("dp")
    me = mp * n_dp + dp
    core, side = lax.rem(mp, 2), mp // 2
    chip = side * n_dp + dp
    sibling = {"mp": mp + 1 - 2 * core, "dp": dp}
    images, tok_count, width = tokens.shape
    every = images * n_dp
    classes = centres.shape[0]
    n_chunk = classes // chunk
    cols = width // n_mp
    half = width // 2
    offset = me * classes
    far_first = [*range(n_dp // 2, n_dp), *range(1, n_dp // 2)]
    log_scale = logit_scale * math.log2(math.e)

    def at_chip(index):
        return {"mp": 2 * (index // n_dp) + core, "dp": lax.rem(index, n_dp)}

    def get_group(index):
        return pltpu.make_async_copy(
            tokens_hbm.at[pl.ds(index * group, group)],
            tokens.at[pl.ds(index * group, group)],
            tok_sem.at[index],
        )

    def get_chunk(index):
        here = pl.ds(pl.multiple_of(index * chunk, chunk), chunk)
        return pltpu.make_async_copy(centres_hbm.at[here], centres.at[here], c_sem.at[index])

    get_win = pltpu.make_async_copy(win_hbm, win, w_sem.at[0])
    get_wout = pltpu.make_async_copy(wout_hbm, wout, w_sem.at[1])
    get_group(0).start()
    get_win.start()
    for index in range(1, images // group):
        get_group(index).start()
    get_wout.start()

    @pl.loop(0, n_chunk)
    def _(index):
        get_chunk(index).start()

    barrier = pltpu.get_barrier_semaphore()

    @pl.loop(1, n_chip)
    def _(step):
        peer = at_chip(lax.rem(chip + step, n_chip))
        pl.semaphore_signal(barrier, inc=1, device_id=peer, device_id_type=MESH)

    @pl.loop(0, n_half)
    def _(step):
        peer = {"mp": 2 * step + 1 - core, "dp": dp}
        pl.semaphore_signal(barrier, inc=1, device_id=peer, device_id_type=MESH)

    label_lane = lax.broadcasted_iota(jnp.int32, (SUBLANES, every), 1)
    own_labels = jnp.zeros((SUBLANES, every), jnp.int32)
    for index in range(images):
        own_labels = jnp.where(label_lane == dp * images + index, labels_ref[index], own_labels)
    lab_out[...] = own_labels

    half_gain = gain_ref[...] * math.sqrt(0.5)

    def norm_group(index):
        get_group(index).wait()
        flat = tokens[index * group : (index + 1) * group].astype(F32)
        return layer_norm(flat.reshape(group * tok_count, width), half_gain).astype(BF16)

    n_group = images // group
    normed = norm_group(0)
    get_win.wait()
    pl.semaphore_wait(barrier, n_chip - 1 + n_half)

    def label_copy(step):
        peer = lax.rem(dp + step, n_dp)
        return pltpu.make_async_remote_copy(
            src_ref=lab_out, dst_ref=labs.at[dp], send_sem=send_sem.at[0], recv_sem=lab_sem,
            device_id={"mp": mp, "dp": peer}, device_id_type=MESH,
        )

    @pl.loop(1, n_dp)
    def _(step):
        label_copy(step).start()

    labs[dp] = own_labels

    for index in range(n_group):
        later = norm_group(index + 1) if index + 1 < n_group else None
        pre = jnp.dot(normed, win[...], preferred_element_type=F32)
        hidden = pre + pre * lax.erf(pre)
        hidden = hidden.reshape(group, tok_count, pre.shape[1])
        hid_sum[index * group : (index + 1) * group, :] = jnp.sum(hidden, axis=1)
        normed = later


    def part_copy(step):
        peer = lax.rem(mp + step, n_mp)
        return pltpu.make_async_remote_copy(
            src_ref=part, dst_ref=part_in.at[mp], send_sem=send_sem.at[1], recv_sem=part_sem,
            device_id={"mp": peer, "dp": dp}, device_id_type=MESH,
        )

    def unit_copy(step):
        peer = lax.rem(dp + step, n_dp)
        return pltpu.make_async_remote_copy(
            src_ref=rows_all.at[core], dst_ref=units.at[core, dp],
            send_sem=send_sem.at[2], recv_sem=unit_sem,
            device_id={"mp": mp, "dp": peer}, device_id_type=MESH,
        )

    def unit_pass():
        return pltpu.make_async_remote_copy(
            src_ref=units.at[core], dst_ref=units.at[core],
            send_sem=send_sem.at[3], recv_sem=fwd_sem,
            device_id=sibling, device_id_type=MESH,
        )

    def stat_swap():
        return pltpu.make_async_remote_copy(
            src_ref=stat_own, dst_ref=stat_pair, send_sem=send_sem.at[4], recv_sem=stat_pair_sem,
            device_id=sibling, device_id_type=MESH,
        )

    def stat_copy(step):
        return pltpu.make_async_remote_copy(
            src_ref=stat_out, dst_ref=stat_in.at[chip], send_sem=send_sem.at[5], recv_sem=stat_sem,
            device_id=at_chip(lax.rem(chip + step, n_chip)), device_id_type=MESH,
        )

    def pick_swap():
        return pltpu.make_async_remote_copy(
            src_ref=pick_pass, dst_ref=pick_pair, send_sem=send_sem.at[6], recv_sem=pick_pair_sem,
            device_id=sibling, device_id_type=MESH,
        )

    def pick_copy(to):
        return pltpu.make_async_remote_copy(
            src_ref=pick_out.at[to // n_dp, lax.rem(to, n_dp)], dst_ref=pick_in.at[chip],
            send_sem=send_sem.at[7], recv_sem=pick_sem,
            device_id=at_chip(to), device_id_type=MESH,
        )

    def grad_swap(to):
        return pltpu.make_async_remote_copy(
            src_ref=grad_pass.at[to], dst_ref=grad_pair.at[to],
            send_sem=send_sem.at[8], recv_sem=grad_pair_sem.at[to],
            device_id=sibling, device_id_type=MESH,
        )

    def grad_copy(to):
        return pltpu.make_async_remote_copy(
            src_ref=grad_out.at[to // n_dp, lax.rem(to, n_dp)], dst_ref=grad_in.at[chip],
            send_sem=send_sem.at[9], recv_sem=grad_sem,
            device_id=at_chip(to), device_id_type=MESH,
        )

    def wait_bytes(ref, count, sem):
        pltpu.make_async_copy(ref.at[pl.ds(0, count)], ref.at[pl.ds(0, count)], sem).wait()

    get_wout.wait()
    hid_mean = hid_sum[...] * (math.sqrt(0.5) / tok_count)
    high = hid_mean.astype(BF16)
    low = (hid_mean - high.astype(F32)).astype(BF16)
    both = jnp.dot(jnp.concatenate([high, low], axis=0), wout[...], preferred_element_type=F32)
    own_part = (both[0:images] + both[images:]).astype(BF16)
    part[...] = own_part

    @pl.loop(1, n_mp)
    def _(step):
        part_copy(lax.rem(step + 1, n_mp - 1) + 1).start()

    part_in[mp] = own_part

    @pl.loop(0, n_group)
    def _(index):
        here = pl.ds(pl.multiple_of(index * group, group), group)
        tok_sum[here, :] = jnp.sum(tokens[here].astype(F32), axis=1)

    ones = jnp.ones((128, 128), BF16)

    def scale_chunk(index, carry):
        get_chunk(index).wait()
        here = pl.ds(pl.multiple_of(index * chunk, chunk), chunk)
        squares = None
        for start in range(0, width, 128):
            piece = centres[here, start : start + 128].astype(F32)
            squares = piece * piece if squares is None else squares + piece * piece
        high = squares.astype(BF16)
        low = (squares - high.astype(F32)).astype(BF16)
        total = jnp.dot(high, ones, preferred_element_type=F32)
        total = total + jnp.dot(low, ones, preferred_element_type=F32)
        scales[here, :] = lax.rsqrt(total + 1e-06) * log_scale
        return carry

    n_first = n_chunk // 2
    lax.fori_loop(0, n_first, scale_chunk, 0)

    wait_bytes(part_in, n_mp - 1, part_sem)
    pooled = tok_sum[...] * (1.0 / tok_count) + jnp.sum(part_in[...].astype(F32), axis=0)
    embedding = layer_norm(pooled, final_ref[...])
    length = jnp.sqrt(jnp.sum(embedding * embedding, axis=1, keepdims=True) + 1e-06)
    own_rows = (embedding / length).astype(BF16)
    rows_all[0] = own_rows[:, 0:half]
    rows_all[1] = own_rows[:, half:]

    for hop in far_first:
        unit_copy(hop).start()

    units[core, dp] = rows_all[core]

    wait_bytes(labs, n_dp - 1, lab_sem)
    label_row = jnp.sum(labs[...], axis=0)[0:1, :] - offset
    label_col = jnp.broadcast_to(label_row.astype(F32), (128, every)).T[:, 0:1].astype(jnp.int32)
    picked_rows[...] = jnp.zeros_like(picked_rows)

    def pick_dot(index):
        here = pl.ds(pl.multiple_of(index * chunk, chunk), chunk)
        lane = lax.broadcasted_iota(jnp.int32, (every, chunk), 1)
        picked = jnp.where(lane == label_col - index * chunk, 1.0, 0.0).astype(BF16)
        return jnp.dot(picked, centres[here, :], preferred_element_type=F32)

    def scale_and_pick(index, carry):
        carry = scale_chunk(index, carry)
        first = pick_dot(index - n_first)
        picked_rows[...] += first + pick_dot(index)
        return carry

    lax.fori_loop(n_first, n_chunk, scale_and_pick, 0)
    own_square = jnp.sum(picked_rows[...] * picked_rows[...], axis=1, keepdims=True)
    own_scale = lax.rsqrt(own_square + 1e-06)

    def pick_block(to_mp):
        here = pl.ds(pl.multiple_of(to_mp * cols, cols), cols)
        return (picked_rows[:, here] * own_scale).astype(BF16).reshape(n_dp, images, cols)

    for to in range(n_half):
        pick_pass[to] = pick_block(2 * to + 1 - core)
    pick_swap().start()

    wait_bytes(units.at[core], n_dp - 1, unit_sem)
    unit_pass().start()

    def place_units(index):
        here = pl.ds(pl.multiple_of(index * half, half), half)
        rows = units[index].reshape(every, half)
        unit_full[:, here] = rows
        unit_t[here, :] = rows.T

    def half_dot(here, index):
        part_of = pl.ds(pl.multiple_of(index * half, half), half)
        return jnp.dot(centres[here, part_of], unit_t[part_of, :], preferred_element_type=F32)

    place_units(core)
    early = raw_half.shape[0]
    raw_half[...] = half_dot(pl.ds(0, early), core)

    pick_swap().wait_recv()
    for to in range(n_half):
        pick_out[to] = pick_block(2 * to + core) + pick_pair[to]

    @pl.loop(1, n_chip)
    def _(step):
        pick_copy(lax.rem(chip + step, n_chip)).start()

    pick_in[chip] = pick_out[side, dp]
    unit_pass().wait_recv()
    place_units(1 - core)

    def weigh(start, count, raw, carry):
        total, inner = carry
        here = pl.ds(start, count)
        scale = scales[here, :]
        if every > 128:
            scale = jnp.concatenate([scale] * (every // 128), axis=1)
        picked = lax.broadcasted_iota(jnp.int32, (count, every), 0) == label_row - start
        exponent = jnp.where(picked, 0.0, jnp.exp2(raw * scale))
        weight = (exponent * scale).astype(BF16)
        weights[:, here] = weight.T
        return (
            total + fold_rows(exponent),
            inner + fold_rows(weight.astype(F32) * raw),
        )

    def class_chunk(index, carry):
        start = early + index * wide
        if not isinstance(start, int):
            start = pl.multiple_of(start, 128)
        raw = jnp.dot(centres[pl.ds(start, wide), :], unit_t[...], preferred_element_type=F32)
        return weigh(start, wide, raw, carry)

    zeros = jnp.zeros((SUBLANES, every), F32)
    raw = raw_half[...] + half_dot(pl.ds(0, early), 1 - core)
    sums = weigh(0, early, raw, (zeros, zeros))
    wide = 3 * early // 2
    n_wide = (classes - early) // wide
    if n_wide <= 2:
        for index in range(n_wide):
            sums = class_chunk(index, sums)
    else:
        sums = lax.fori_loop(0, n_wide, class_chunk, sums)
    total, inner = sums
    target = jnp.zeros((every, 128), F32)
    for start in range(0, width, 128):
        picked = (picked_rows[:, start : start + 128] * own_scale).astype(BF16).astype(F32)
        target = target + unit_full[:, start : start + 128].astype(F32) * picked
    stat_own[0:1, :] = jnp.sum(total, axis=0, keepdims=True)
    stat_own[1:2, :] = jnp.sum(inner, axis=0, keepdims=True)
    stat_own[2:3, :] = jnp.sum(target.T, axis=0, keepdims=True)
    stat_own[3:4, :] = jnp.zeros((1, every), F32)
    stat_swap().start()

    def grad_block(to_mp):
        here = pl.ds(pl.multiple_of(to_mp * cols, cols), cols)
        return jnp.dot(weights[...], centres[:, here], preferred_element_type=F32)

    def pass_cols(step, carry):
        to = lax.rem(side + 1 + step, n_half)
        grad_pass[to] = grad_block(2 * to + 1 - core).astype(BF16).reshape(n_dp, images, cols)
        grad_swap(to).start()
        return carry

    lax.fori_loop(0, n_half, pass_cols, 0)
    stat_swap().wait_recv()
    chip_stats = stat_own[...] + stat_pair[...]
    stat_out[...] = chip_stats

    @pl.loop(1, n_chip)
    def _(step):
        stat_copy(step).start()

    stat_in[chip] = chip_stats

    def send_cols(step, carry):
        to = lax.rem(side + 1 + step, n_half)
        grad_swap(to).wait_recv()
        block = grad_block(2 * to + core) + grad_pair[to].reshape(every, cols).astype(F32)
        grad_out[to] = block.astype(BF16).reshape(n_dp, images, cols)

        for hop in far_first:
            grad_copy(to * n_dp + lax.rem(dp + hop, n_dp)).start()

        @pl.when(to != side)
        def _():
            grad_copy(to * n_dp + dp).start()

        return carry

    lax.fori_loop(0, n_half, send_cols, 0)
    grad_in[chip] = grad_out[side, dp]

    @pl.loop(1, n_mp)
    def _(step):
        part_copy(step).wait_send()

    @pl.loop(1, n_dp)
    def _(step):
        label_copy(step).wait_send()
        unit_copy(step).wait_send()

    unit_pass().wait_send()
    stat_swap().wait_send()
    pick_swap().wait_send()

    @pl.loop(0, n_half)
    def _(to):
        grad_swap(to).wait_send()

    @pl.loop(1, n_chip)
    def _(step):
        stat_copy(step).wait_send()
        pick_copy(lax.rem(chip + step, n_chip)).wait_send()

    wait_bytes(stat_in, n_chip - 1, stat_sem)
    stat_sum[...] = jnp.zeros_like(stat_sum)
    stat_sum[0:STATS, :] = jnp.sum(stat_in[...], axis=0)
    picked_rows[:, 0:128] = stat_sum[...].T
    stats = picked_rows[pl.ds(pl.multiple_of(dp * images, images), images), 0:128]
    others, inner_sum, target_cos = stats[:, 0:1], stats[:, 1:2], stats[:, 2:3]
    shifted, slope = arc_target(target_cos)
    target_exp = jnp.exp(logit_scale * shifted)
    totals = others + target_exp
    rate = logit_scale / totals
    target_weight = (logit_scale * ((target_exp / totals - 1.0) * slope)).astype(BF16).astype(F32)
    rate = rate * (1.0 / log_scale)
    inner_all = rate * inner_sum + target_weight * target_cos
    diagonal = lax.broadcasted_iota(jnp.int32, (images, images), 0) == lax.broadcasted_iota(
        jnp.int32, (images, images), 1
    )
    row_loss = jnp.log(totals) - logit_scale * shifted
    loss_ref[...] = jnp.sum(jnp.where(diagonal, row_loss, 0.0), axis=0, keepdims=True)
    unit_here = unit_full[
        pl.ds(pl.multiple_of(dp * images, images), images),
        pl.ds(pl.multiple_of(mp * cols, cols), cols),
    ].astype(F32)
    wait_bytes(pick_in, n_chip - 1, pick_sem)
    centre_rows = jnp.sum(pick_in[...].astype(F32), axis=0)
    rest = target_weight * centre_rows - unit_here * inner_all
    wait_bytes(grad_in, n_chip - 1, grad_sem)
    gathered = jnp.sum(grad_in[...].astype(F32), axis=0)
    grad_ref[...] = (gathered * rate + rest) / length

    @pl.loop(1, n_chip)
    def _(step):
        peer = lax.rem(chip + step, n_chip)
        grad_copy(peer).wait_send()


def shards(n_mp, n_dp, tokens, norm_gain, weight_in, weight_out, final_gain, centres, labels):
    images, tok_count, width = tokens.shape
    hidden = weight_in.shape[1]
    classes = centres.shape[0]
    every = images * n_dp
    n_half = n_mp // 2
    n_chip = n_half * n_dp
    cols = width // n_mp
    chunk = min(1024, classes)
    group = 8
    any_spec = pl.BlockSpec(memory_space=pltpu.HBM)
    vmem_spec = pl.BlockSpec(memory_space=pltpu.VMEM)
    loss, grad = pl.pallas_call(
        functools.partial(kernel, n_mp, n_dp, chunk, group),
        out_shape=(
            jax.ShapeDtypeStruct((1, images), F32),
            jax.ShapeDtypeStruct((images, cols), F32),
        ),
        in_specs=[any_spec, vmem_spec, any_spec, any_spec, vmem_spec, any_spec,
            pl.BlockSpec(memory_space=pltpu.SMEM)],
        out_specs=(vmem_spec, vmem_spec),
        scratch_shapes=[
            pltpu.VMEM((images, tok_count, width), BF16),
            pltpu.VMEM((width, hidden), BF16),
            pltpu.VMEM((hidden, width), BF16),
            pltpu.VMEM((classes, width), BF16),
            pltpu.VMEM((n_dp, SUBLANES, every), jnp.int32),
            pltpu.VMEM((images, hidden), F32),
            pltpu.VMEM((images, width), F32),
            pltpu.VMEM((images, width), BF16),
            pltpu.VMEM((n_mp, images, width), BF16),
            pltpu.VMEM((2, n_dp, images, width // 2), BF16),
            pltpu.VMEM((every, width), BF16),
            pltpu.VMEM((width, every), BF16),
            pltpu.VMEM((classes // 4 * 128 // every, every), F32),
            pltpu.VMEM((2, images, width // 2), BF16),
            pltpu.VMEM((classes, 128), F32),
            pltpu.VMEM((every, width), F32),
            pltpu.VMEM((every, classes), BF16),
            pltpu.VMEM((STATS, every), F32),
            pltpu.VMEM((STATS, every), F32),
            pltpu.VMEM((STATS, every), F32),
            pltpu.VMEM((n_chip, STATS, every), F32),
            pltpu.VMEM((128, every), F32),
            pltpu.VMEM((n_half, n_dp, images, cols), BF16),
            pltpu.VMEM((n_half, n_dp, images, cols), BF16),
            pltpu.VMEM((n_half, n_dp, images, cols), BF16),
            pltpu.VMEM((n_chip, images, cols), BF16),
            pltpu.VMEM((n_half, n_dp, images, cols), BF16),
            pltpu.VMEM((n_half, n_dp, images, cols), BF16),
            pltpu.VMEM((n_half, n_dp, images, cols), BF16),
            pltpu.VMEM((n_chip, images, cols), BF16),
            pltpu.VMEM((SUBLANES, every), jnp.int32),
            pltpu.SemaphoreType.DMA((images // group,)),
            pltpu.SemaphoreType.DMA((2,)),
            pltpu.SemaphoreType.DMA((classes // chunk,)),
            pltpu.SemaphoreType.DMA((10,)),
            pltpu.SemaphoreType.DMA,
            pltpu.SemaphoreType.DMA,
            pltpu.SemaphoreType.DMA,
            pltpu.SemaphoreType.DMA,
            pltpu.SemaphoreType.DMA,
            pltpu.SemaphoreType.DMA,
            pltpu.SemaphoreType.DMA,
            pltpu.SemaphoreType.DMA,
            pltpu.SemaphoreType.DMA((n_half,)),
            pltpu.SemaphoreType.DMA,
        ],
        compiler_params=pltpu.CompilerParams(
            collective_id=0, has_side_effects=True, vmem_limit_bytes=56 * 1024 * 1024
        ),
    )(
        tokens, norm_gain.reshape(1, width), weight_in, weight_out,
        final_gain.reshape(1, width), centres, labels,
    )
    def emit(loss_in, grad_in, loss_out, grad_out):
        loss_out[...] = loss_in[...]
        grad_out[...] = grad_in[...]

    loss, grad = pl.pallas_call(
        emit,
        out_shape=(
            jax.ShapeDtypeStruct((1, images), F32),
            jax.ShapeDtypeStruct((images, cols), F32),
        ),
        in_specs=[vmem_spec, vmem_spec],
        out_specs=(vmem_spec, vmem_spec),
    )(loss, grad)
    return (loss.reshape(images), grad)


def solution(mesh):
    return jax.shard_map(
        functools.partial(shards, mesh.shape["mp"], mesh.shape["dp"]),
        mesh=mesh,
        in_specs=(
            P("dp", None, None),
            P(),
            P(None, "mp"),
            P("mp", None),
            P(),
            P(("mp", "dp"), None),
            P("dp"),
        ),
        out_specs=(P("dp"), P("dp", "mp")),
        check_vma=False,
    )
```
